512 devices in a mesh: wide: 128 (over x_lo, y, z), narrow: 4 (over x_hi, core).
Axes of the slice: x: 4 (x_hi: 2, x_lo: 2; x = x_hi * 2 + x_lo), y: 4, z: 16, core: 2. Of those that a mesh axis runs over, the one named last changes fastest.
Arguments:
- raw_ints: bfloat16 [4, 640, 128, 2, 384], P('narrow', 'wide'), may hold values from -5 to 5
- metric_root: bfloat16 [640, 640], P('wide'), may hold values from -0.25 to 0.25
- occ_energy: float32 [8, 2], replicated, may hold values from -1.6 to -0.4
- vir_energy: float32 [4, 384], replicated, may hold values from 0.3 to 2.5
- block_kpoint: int32 [4, 128], replicated, may hold values from 0 to 7
- occ_count: int32 [4, 128], replicated, may hold values from 1 to 2, as said below
Outputs:
- gamma: bfloat16 [4, 640, 128, 2, 384], P('narrow', None, 'wide')
- virt_density: float32 [147456], P(('wide', 'narrow'))
The draws below stay inside these ranges and needn't reach their ends.
Inputs may be any that keep to these rules, and one draw needn't show every extreme that they name: `occ_count`: slot o of a block is live when o is less than its count; some block has all 2 slots live.
All inputs are finite; a program needn't handle non-finite values.
Results may differ from the reference program's by a relative error of at most 0.0043.
Values may be sent and summed in bfloat16 or wider, within the bound.
A program may use at most 64 MiB of HBM per device.

```python
import jax
import jax.numpy as jnp
from jax import lax

NAUX = 640
V = 384
OCC = 2
WINDOW = 3
NKPT = 8
BLOCKS = 128
KGROUPS = 4


def draw_occ_count(key, part):
    first_key = jax.random.fold_in(key, 11)
    second_key = jax.random.fold_in(key, 23)
    counts = jax.random.randint(first_key, (KGROUPS * BLOCKS,), 1, OCC + 1)
    chosen = jax.random.randint(second_key, (), 0, KGROUPS * BLOCKS)
    counts = counts.at[chosen].set(OCC)
    return counts.reshape(KGROUPS, BLOCKS).astype(jnp.int32)


def draw_raw_ints(key, part):
    noise_key = jax.random.fold_in(key, 101)
    sign_key = jax.random.fold_in(key, 103)
    profile_key = jax.random.fold_in(key, 107)
    phase_key = jax.random.fold_in(key, 109)
    pairing_key = jax.random.fold_in(key, 113)
    full_shape = (KGROUPS, NAUX, BLOCKS, OCC, V)
    noise = jnp.clip(0.15 * jax.random.normal(noise_key, full_shape, jnp.float32), -0.9, 0.9)
    profiles = jnp.clip(jax.random.normal(profile_key, (2, V), jnp.float32), -3.0, 3.0)
    slice_rows = NAUX // BLOCKS
    pairing = jax.random.permutation(pairing_key, BLOCKS)
    slice_index = jnp.arange(NAUX, dtype=jnp.int32) // slice_rows
    spiked = pairing[slice_index][:, None] == jnp.arange(BLOCKS, dtype=jnp.int32)[None, :]
    boost = jnp.where(spiked, 5.0, 1.0).astype(jnp.float32)
    signs = jax.random.randint(sign_key, (KGROUPS, NAUX, BLOCKS, OCC), 0, 2).astype(jnp.float32) * 2.0 - 1.0
    phase = jax.random.randint(phase_key, (), 0, 8).astype(jnp.float32) * (jnp.pi / 4.0)
    angle = phase + jnp.pi / 4.0 * jnp.arange(BLOCKS, dtype=jnp.float32)
    profile = jnp.cos(angle)[:, None] * profiles[0][None, :] + jnp.sin(angle)[:, None] * profiles[1][None, :]
    values = noise * boost[None, :, :, None, None] + 0.2 * signs[..., None] * profile[None, None, :, None, :]
    return jnp.clip(values, -5.0, 5.0).astype(jnp.bfloat16)


def plant(array, stream_key, least, top_value):
    longest = array.shape.index(max(array.shape))
    spots = []
    for shift in (0, 1):
        where = [jax.random.randint(jax.random.fold_in(stream_key, axis), (), 0, length) for axis, length in enumerate(array.shape)]
        where[longest] = (where[longest] + shift) % array.shape[longest]
        spots.append(tuple(where))
    return array.at[spots[0]].set(least).at[spots[1]].set(top_value)


def shard_levels(key, shape, shards, least, largest):
    def one(dim, parts):
        steps = jax.random.uniform(jax.random.fold_in(jax.random.fold_in(key, 6), dim), (parts,), jnp.float32, least / len(shards), largest / len(shards))
        return jnp.repeat(jnp.exp(steps), shape[dim] // parts).reshape((-1,) + (1,) * (len(shape) - dim - 1))

    level = one(*shards[0])
    for cut in shards[1:]:
        level = level * one(*cut)
    return level


def centred(own_key, dims, scale, bound, split=(), kind=jnp.bfloat16):
    drawn = jax.random.normal(own_key, dims, jnp.float32) * scale
    if len(split) > 0:
        drawn = shard_levels(own_key, dims, split, -0.22, 0.18) * drawn
    return jnp.clip(drawn, min=-bound, max=bound).astype(kind)


def setup_inputs(seed: int = 0) -> dict:
    splits = jax.random.split(jax.random.key(seed), 7)
    raw_ints = draw_raw_ints(jax.random.fold_in(splits[6], 71), 0)
    metric_root = centred(splits[1], (NAUX, NAUX), NAUX ** -0.5, 0.25, ((0, 128),))
    occ_energy = jnp.clip(jax.random.uniform(splits[2], (NKPT, OCC), jnp.float32, -1.6, -0.4), -1.6, -0.4)
    vir_energy = jnp.clip(jax.random.uniform(splits[3], (KGROUPS, V), jnp.float32, 0.3, 2.5), 0.3, 2.5)
    block_kpoint = plant(jax.random.randint(splits[4], (KGROUPS, BLOCKS), 0, NKPT), jax.random.fold_in(splits[4], 1), 0, NKPT - 1).astype(jnp.int32)
    occ_count = draw_occ_count(jax.random.fold_in(splits[6], 71), 0)
    return {"raw_ints": raw_ints, "metric_root": metric_root, "occ_energy": occ_energy, "vir_energy": vir_energy, "block_kpoint": block_kpoint, "occ_count": occ_count}


def reference(raw_ints, metric_root, occ_energy, vir_energy, block_kpoint, occ_count):
    group_count, aux_count, block_count, occ_slots, vir_count = raw_ints.shape
    row_width = occ_slots * vir_count
    stacked = []
    for group_id in range(group_count):
        aux_rows = raw_ints[group_id].reshape(aux_count, block_count * row_width)
        product = lax.dot_general(metric_root, aux_rows, (((0,), (0,)), ((), ())), preferred_element_type=jnp.float32)
        stacked.append(product.astype(jnp.bfloat16).reshape(aux_count, block_count, row_width))
    fitted = jnp.stack(stacked)
    occ_block = occ_energy[block_kpoint]
    live = (jnp.arange(occ_slots, dtype=jnp.int32)[None, None, :] < occ_count[:, :, None]).astype(jnp.float32)
    norm_scale = 1.0 / (group_count * block_count * vir_count)

    def one_block(density, position):
        group_id = position // block_count
        my_block = position % block_count
        partner_group = (group_id + group_count // 2) % group_count
        own_rows = fitted[group_id, :, my_block]
        vir_own = vir_energy[group_id]
        vir_partner = vir_energy[partner_group]
        occ_own = occ_block[group_id, my_block]
        live_own = live[group_id, my_block]
        gamma_sum = jnp.zeros((aux_count, row_width), jnp.float32)
        for offset in range(WINDOW):
            other_block = (my_block + offset) % block_count
            far_rows = fitted[partner_group, :, other_block]
            coulomb = lax.dot_general(own_rows, far_rows, (((0,), (0,)), ((), ())), preferred_element_type=jnp.float32)
            coulomb = coulomb.reshape(occ_slots, vir_count, occ_slots, vir_count)
            denominator = (occ_own[:, None, None, None] + occ_block[partner_group, other_block][None, None, :, None]
                           - vir_own[None, :, None, None] - vir_partner[None, None, None, :])
            amplitude = coulomb / denominator * live_own[:, None, None, None] * live[partner_group, other_block][None, None, :, None]
            mixed_amp = 2.0 * amplitude - jnp.transpose(amplitude, (0, 3, 2, 1))
            amp_half = amplitude.astype(jnp.bfloat16)
            mixed_half = mixed_amp.astype(jnp.bfloat16)
            gamma_sum = gamma_sum + lax.dot_general(far_rows, mixed_half.reshape(row_width, row_width), (((1,), (1,)), ((), ())), preferred_element_type=jnp.float32)
            density = density + jnp.einsum('iajc,ibjc->ab', mixed_half.astype(jnp.float32), amp_half.astype(jnp.float32))
        return density, gamma_sum.astype(jnp.bfloat16)

    density, gammas = lax.scan(one_block, jnp.zeros((vir_count, vir_count), jnp.float32), jnp.arange(group_count * block_count, dtype=jnp.int32))
    gamma = gammas.reshape(group_count, block_count, aux_count, occ_slots, vir_count).transpose(0, 2, 1, 3, 4)
    return gamma, (density * norm_scale).reshape(-1)
```

```python
import functools

import jax
import jax.numpy as jnp
from jax import lax
from jax.experimental import pallas as pl
from jax.experimental.pallas import tpu as pltpu
from jax.sharding import Mesh
from jax.sharding import PartitionSpec as P

MESH_ID = pl.DeviceIdType.MESH


def coords(w, n):
    x, y, z = split_wide(w)
    return (x, y, z, n // 2, n % 2)


def split_wide(w):
    return w // 64, (w // 16) % 4, w % 16


def join_wide(x, y, z):
    return x * 64 + y * 16 + z


def slot_of(w):
    x, y, z = split_wide(w)
    return x * 64 + y * 16 + (z % 2) * 8 + z // 2


def peer_at(step, w):
    x, y, z = split_wide(w)
    turn, side = step // 8, step % 8
    half = (turn + 1) // 2
    dz = jnp.where(turn % 2 == 1, half, 16 - half)
    return join_wide((x + side // 4) % 2, (y + side % 4) % 4, (z + dz) % 16)


def regroup_kernel(raw, root, recv, metric, ssem, rsem, msend, mrecv):
    w = lax.axis_index(WIDE)
    n = lax.axis_index(NARROW)
    core = n % 2
    sibling = n + 1 - 2 * core
    x, y, z = split_wide(w)
    barrier = pltpu.get_barrier_semaphore()

    def greet(step, carry):
        pl.semaphore_signal(barrier, inc=1, device_id=coords((w + step) % 128, n), device_id_type=MESH_ID)
        return carry

    lax.fori_loop(1, 128, greet, 0)
    pl.semaphore_signal(barrier, inc=1, device_id=coords(w, sibling), device_id_type=MESH_ID)
    pl.semaphore_wait(barrier, 128)

    mine = slot_of(w)
    par = (z + core) % 2

    def send_metric(step, carry):
        dz = 2 * step + core

        @pl.when(dz != 0)
        def _():
            pltpu.make_async_remote_copy(
                root, metric.at[mine], msend.at[0], mrecv.at[0],
                device_id=coords(join_wide(x, y, (z + dz) % 16), n), device_id_type=MESH_ID,
            ).start()

        @pl.when(dz == 0)
        def _():
            pltpu.make_async_copy(root, metric.at[mine], mrecv.at[0]).start()

        return carry

    lax.fori_loop(0, 8, send_metric, 0)
    pltpu.make_async_copy(raw.at[0, :, w], recv.at[mine], rsem).start()

    def send_raw(step, carry):
        peer = peer_at(step, w)

        @pl.when(peer != w)
        def _():
            pltpu.make_async_remote_copy(
                raw.at[0, :, peer], recv.at[mine], ssem, rsem, device_id=coords(peer, n), device_id_type=MESH_ID
            ).start()

        return carry

    lax.fori_loop(0, 128, send_raw, 0)

    line = metric.at[pl.ds(pl.multiple_of(x * 64 + y * 16 + par * 8, 8), 8)]
    pltpu.make_async_copy(line, line, mrecv.at[0]).wait()
    for step in range(1, 4):
        pltpu.make_async_remote_copy(
            line, line, msend.at[1], mrecv.at[1],
            device_id=coords(join_wide(x, (y + step) % 4, z), n), device_id_type=MESH_ID,
        ).start()
    three = metric.at[pl.ds(0, 24)]
    pltpu.make_async_copy(three, three, mrecv.at[1]).wait()
    copies = []
    for row in range(4):
        part = metric.at[pl.ds(pl.multiple_of(x * 64 + row * 16 + par * 8, 8), 8)]
        copies.append(pltpu.make_async_remote_copy(
            part, part, msend.at[2], mrecv.at[2],
            device_id=coords(join_wide(1 - x, y, z), n), device_id_type=MESH_ID,
        ))
    for copy in copies:
        copy.start()
    four = metric.at[pl.ds(0, 32)]
    pltpu.make_async_copy(four, four, mrecv.at[2]).wait()
    for row in range(8):
        part = metric.at[pl.ds(pl.multiple_of(row * 16 + par * 8, 8), 8)]
        pltpu.make_async_remote_copy(
            part, part, msend.at[3], mrecv.at[3], device_id=coords(w, sibling), device_id_type=MESH_ID
        ).start()
    eight = metric.at[pl.ds(0, 64)]
    pltpu.make_async_copy(eight, eight, mrecv.at[3]).wait()

    @pl.when(core == 0)
    def _():
        part = metric.at[pl.ds(0, 7)]
        pltpu.make_async_copy(part, part, msend.at[0]).wait()

    @pl.when(core == 1)
    def _():
        part = metric.at[pl.ds(0, 8)]
        pltpu.make_async_copy(part, part, msend.at[0]).wait()

    pltpu.make_async_copy(three, three, msend.at[1]).wait()
    pltpu.make_async_copy(four, four, msend.at[2]).wait()
    pltpu.make_async_copy(eight, eight, msend.at[3]).wait()
    others = recv.at[pl.ds(0, 127)]
    pltpu.make_async_copy(others, others, ssem).wait()
    pltpu.make_async_copy(recv, recv, rsem).wait()


def regroup(raw_ints, metric_root):
    rows, cols = metric_root.shape
    return pl.pallas_call(
        regroup_kernel,
        name="regroup",
        out_shape=(
            jax.ShapeDtypeStruct((128,) + raw_ints.shape[1:2] + raw_ints.shape[3:], jnp.bfloat16),
            jax.ShapeDtypeStruct((128, rows, cols), jnp.bfloat16),
        ),
        in_specs=[pl.BlockSpec(memory_space=pltpu.VMEM)] * 2,
        out_specs=(pl.BlockSpec(memory_space=pltpu.VMEM),) * 2,
        scratch_shapes=[
            pltpu.SemaphoreType.DMA,
            pltpu.SemaphoreType.DMA,
            pltpu.SemaphoreType.DMA((4,)),
            pltpu.SemaphoreType.DMA((4,)),
        ],
        compiler_params=pltpu.CompilerParams(collective_id=0, has_side_effects=True),
    )(raw_ints, metric_root)


WINDOW = 3
WIDE = ("wide_0", "wide_1", "wide_2")
NARROW = ("narrow_0", "narrow_1")
WIDE_NARROW = ("wide_0", "wide_1", "wide_2", "narrow_0", "narrow_1")


def in_order(parts, dim):
    parts = jnp.moveaxis(parts, 0, dim)
    dims = parts.shape
    return parts.reshape(*dims[:dim], dims[dim] * dims[dim + 1], *dims[dim + 2 :])


def gather_in_order(array, axes, order):
    parts = array
    for k in order:
        parts = lax.all_gather(parts, axes[k])
    done = order[::-1]
    back = [done.index(k) for k in range(len(axes))]
    parts = parts.transpose(*back, *range(len(axes), parts.ndim))
    return parts.reshape(-1, *array.shape)


def gather_axes(array, axes, order, dim):
    return in_order(gather_in_order(array, axes, order), dim)


def from_behind(value, axis, steps):
    count = lax.axis_size(axis)
    pairs = [(source, (source + steps) % count) for source in range(count)]
    return lax.ppermute(value, axis, pairs)


def partner(value, axis, bit):
    mask = 2**bit
    pairs = [(source, source ^ mask) for source in range(lax.axis_size(axis))]
    return lax.ppermute(value, axis, pairs)


def cut_along(array, dim, peers):
    before, after = (array.shape[:dim], array.shape[dim + 1 :])
    return jnp.moveaxis(array.reshape(*before, peers, -1, *after), dim, 0)


def scatter_pairs(array, chips, core, dim):
    sizes = (lax.axis_size(chips), lax.axis_size(core))
    parts = cut_along(array, dim, sizes[0] * sizes[1])
    inside = parts.shape[1:]
    parts = parts.reshape(*sizes, *inside).swapaxes(0, 1).reshape(-1, *inside)
    parts = lax.psum_scatter(parts, core, scatter_dimension=0, tiled=True)
    return lax.psum_scatter(parts, chips, scatter_dimension=0, tiled=True)[0]


def shards(raw_ints, metric_root, occ_energy, vir_energy, block_kpoint, occ_count):
    occ_slots = raw_ints.shape[3]
    vir_count = raw_ints.shape[4]
    row_width = occ_slots * vir_count
    wide_count = lax.axis_size(WIDE)
    group_count = lax.axis_size(NARROW)
    my_block = lax.axis_index(WIDE)
    my_group = lax.axis_index(NARROW)
    partner_group = (my_group + group_count // 2) % group_count
    flip_bit = group_count.bit_length() - 2
    blocks, roots = regroup(raw_ints, metric_root)
    aux_count = wide_count * metric_root.shape[0]
    fitted = lax.dot_general(
        roots.reshape(aux_count, aux_count),
        blocks.reshape(aux_count, row_width),
        (((0,), (0,)), ((), ())),
        preferred_element_type=jnp.float32,
    ).astype(jnp.bfloat16)

    def window_blocks(source):
        shifted = [from_behind(source, WIDE, -offset) for offset in range(1, WINDOW)]
        return shifted

    paired = [
        partner(own_piece, NARROW, flip_bit) for own_piece in [fitted] + window_blocks(fitted)
    ]

    def block_state(group_index, block_index):
        k_point = lax.dynamic_slice(block_kpoint, (group_index, block_index), (1, 1))[0, 0]
        picked = jnp.sum(
            jnp.where(jnp.arange(occ_energy.shape[0])[:, None] == k_point, occ_energy, 0.0), axis=0
        )
        live_count = lax.dynamic_slice(occ_count, (group_index, block_index), (1, 1))[0, 0]
        live_slots = (jnp.arange(occ_slots) < live_count).astype(jnp.float32)
        return (picked, live_slots)

    vir_own = lax.dynamic_index_in_dim(vir_energy, my_group, 0, keepdims=False)
    vir_partner = lax.dynamic_index_in_dim(vir_energy, partner_group, 0, keepdims=False)
    occ_own, live_own = block_state(my_group, my_block)
    gamma_sum = jnp.zeros((aux_count, row_width), jnp.float32)
    density = jnp.zeros((vir_count, vir_count), jnp.float32)
    for offset in range(WINDOW):
        far_rows = paired[offset]
        occ_other, live_other = block_state(partner_group, (my_block + offset) % wide_count)
        coulomb = lax.dot_general(
            fitted, far_rows, (((0,), (0,)), ((), ())), preferred_element_type=jnp.float32
        )
        coulomb = coulomb.reshape(occ_slots, vir_count, occ_slots, vir_count)
        denominator = (
            occ_own[:, None, None, None]
            + occ_other[None, None, :, None]
            - vir_own[None, :, None, None]
            - vir_partner[None, None, None, :]
        )
        amplitude = (
            coulomb / denominator * live_own[:, None, None, None] * live_other[None, None, :, None]
        )
        mixed_amp = 2.0 * amplitude - jnp.transpose(amplitude, (0, 3, 2, 1))
        amp_half = amplitude.astype(jnp.bfloat16)
        mixed_half = mixed_amp.astype(jnp.bfloat16)
        gamma_sum = gamma_sum + lax.dot_general(
            far_rows,
            mixed_half.reshape(row_width, row_width),
            (((1,), (1,)), ((), ())),
            preferred_element_type=jnp.float32,
        )
        density = density + jnp.einsum(
            "iajc,ibjc->ab", mixed_half, amp_half, preferred_element_type=jnp.float32
        )
    norm_scale = 1.0 / (group_count * wide_count * vir_count)
    virt_density = (
        scatter_pairs(
            density.reshape(-1), ("wide_0", "wide_1", "wide_2", "narrow_0"), "narrow_1", 0
        )
        * norm_scale
    )
    return (
        gamma_sum.astype(jnp.bfloat16).reshape(1, aux_count, 1, occ_slots, vir_count),
        virt_density,
    )


def solution(mesh):
    torus = Mesh(
        mesh.devices.reshape(2, 4, 16, 2, 2), ("wide_0", "wide_1", "wide_2", "narrow_0", "narrow_1")
    )
    placed = (P(NARROW, WIDE, None, None, None), P(WIDE, None), P(), P(), P(), P())
    return jax.shard_map(
        shards,
        mesh=torus,
        in_specs=placed,
        out_specs=(P(NARROW, None, WIDE, None, None), P(WIDE_NARROW)),
        check_vma=False,
    )
```

```python
import functools

import jax
import jax.numpy as jnp
from jax import lax
from jax.experimental import pallas as pl
from jax.experimental.pallas import tpu as pltpu

from jax.sharding import PartitionSpec as P

MESH_ID = pl.DeviceIdType.MESH


def split_wide(w):
    return w // 64, (w // 16) % 4, w % 16


def join_wide(x, y, z):
    return x * 64 + y * 16 + z


def slot_of(w):
    x, y, z = split_wide(w)
    return x * 64 + y * 16 + (z % 2) * 8 + z // 2


def peer_at(step, w):
    x, y, z = split_wide(w)
    turn, side = step // 8, step % 8
    half = (turn + 1) // 2
    dz = jnp.where(turn % 2 == 1, half, 16 - half)
    return join_wide((x + side // 4) % 2, (y + side % 4) % 4, (z + dz) % 16)


def regroup_kernel(raw, root, recv, metric, ssem, rsem, msend, mrecv):
    w = lax.axis_index("wide")
    n = lax.axis_index("narrow")
    core = n % 2
    sibling = n + 1 - 2 * core
    x, y, z = split_wide(w)
    barrier = pltpu.get_barrier_semaphore()

    def greet(step, carry):
        pl.semaphore_signal(barrier, inc=1, device_id=((w + step) % 128, n), device_id_type=MESH_ID)
        return carry

    lax.fori_loop(1, 128, greet, 0)
    pl.semaphore_signal(barrier, inc=1, device_id=(w, sibling), device_id_type=MESH_ID)
    pl.semaphore_wait(barrier, 128)

    mine = slot_of(w)
    par = (z + core) % 2

    def send_metric(step, carry):
        dz = 2 * step + core

        @pl.when(dz != 0)
        def _():
            pltpu.make_async_remote_copy(
                root, metric.at[mine], msend.at[0], mrecv.at[0],
                device_id=(join_wide(x, y, (z + dz) % 16), n), device_id_type=MESH_ID,
            ).start()

        @pl.when(dz == 0)
        def _():
            pltpu.make_async_copy(root, metric.at[mine], mrecv.at[0]).start()

        return carry

    lax.fori_loop(0, 8, send_metric, 0)
    pltpu.make_async_copy(raw.at[0, :, w], recv.at[mine], rsem).start()

    def send_raw(step, carry):
        peer = peer_at(step, w)

        @pl.when(peer != w)
        def _():
            pltpu.make_async_remote_copy(
                raw.at[0, :, peer], recv.at[mine], ssem, rsem, device_id=(peer, n), device_id_type=MESH_ID
            ).start()

        return carry

    lax.fori_loop(0, 128, send_raw, 0)

    line = metric.at[pl.ds(pl.multiple_of(x * 64 + y * 16 + par * 8, 8), 8)]
    pltpu.make_async_copy(line, line, mrecv.at[0]).wait()
    for step in range(1, 4):
        pltpu.make_async_remote_copy(
            line, line, msend.at[1], mrecv.at[1],
            device_id=(join_wide(x, (y + step) % 4, z), n), device_id_type=MESH_ID,
        ).start()
    three = metric.at[pl.ds(0, 24)]
    pltpu.make_async_copy(three, three, mrecv.at[1]).wait()
    copies = []
    for row in range(4):
        part = metric.at[pl.ds(pl.multiple_of(x * 64 + row * 16 + par * 8, 8), 8)]
        copies.append(pltpu.make_async_remote_copy(
            part, part, msend.at[2], mrecv.at[2],
            device_id=(join_wide(1 - x, y, z), n), device_id_type=MESH_ID,
        ))
    for copy in copies:
        copy.start()
    four = metric.at[pl.ds(0, 32)]
    pltpu.make_async_copy(four, four, mrecv.at[2]).wait()
    for row in range(8):
        part = metric.at[pl.ds(pl.multiple_of(row * 16 + par * 8, 8), 8)]
        pltpu.make_async_remote_copy(
            part, part, msend.at[3], mrecv.at[3], device_id=(w, sibling), device_id_type=MESH_ID
        ).start()
    eight = metric.at[pl.ds(0, 64)]
    pltpu.make_async_copy(eight, eight, mrecv.at[3]).wait()

    @pl.when(core == 0)
    def _():
        part = metric.at[pl.ds(0, 7)]
        pltpu.make_async_copy(part, part, msend.at[0]).wait()

    @pl.when(core == 1)
    def _():
        part = metric.at[pl.ds(0, 8)]
        pltpu.make_async_copy(part, part, msend.at[0]).wait()

    pltpu.make_async_copy(three, three, msend.at[1]).wait()
    pltpu.make_async_copy(four, four, msend.at[2]).wait()
    pltpu.make_async_copy(eight, eight, msend.at[3]).wait()
    others = recv.at[pl.ds(0, 127)]
    pltpu.make_async_copy(others, others, ssem).wait()
    pltpu.make_async_copy(recv, recv, rsem).wait()


def regroup(raw_ints, metric_root):
    rows, cols = metric_root.shape
    return pl.pallas_call(
        regroup_kernel,
        name="regroup",
        out_shape=(
            jax.ShapeDtypeStruct((128,) + raw_ints.shape[1:2] + raw_ints.shape[3:], jnp.bfloat16),
            jax.ShapeDtypeStruct((128, rows, cols), jnp.bfloat16),
        ),
        in_specs=[pl.BlockSpec(memory_space=pltpu.VMEM)] * 2,
        out_specs=(pl.BlockSpec(memory_space=pltpu.VMEM),) * 2,
        scratch_shapes=[
            pltpu.SemaphoreType.DMA,
            pltpu.SemaphoreType.DMA,
            pltpu.SemaphoreType.DMA((4,)),
            pltpu.SemaphoreType.DMA((4,)),
        ],
        compiler_params=pltpu.CompilerParams(collective_id=0, has_side_effects=True),
    )(raw_ints, metric_root)


CHUNKS = 5
WINDOW = 3


def add_up(ref, count):
    total = ref[0]
    for k in range(1, count):
        total = total + ref[k]
    return total


def pair_kernel(
    own, own_t, vir, occ, kpoint, count,
    gamma, piece,
    relay, far, table, column, total, dens, amp, mix,
    core_in, y_out, y_in, z_sum, z_out, z_in, x_out, x_in,
    own_sent, relay_in, relay_sent, near_in, near_sent, next_in, next_sent, last_in, dsend, drecv,
):
    aux, width = own.shape
    nvir = vir.shape[1]
    half_rows = aux // 2
    rows = half_rows // CHUNKS
    w = lax.axis_index("wide")
    n = lax.axis_index("narrow")
    core, x_hi = n % 2, n // 2
    x_lo, y, z = split_wide(w)
    x = 2 * x_hi + x_lo
    ahead, behind = (w + 127) % 128, (w + 1) % 128

    def along_x(step):
        there = (x + step) % 4
        return join_wide(there % 2, y, z), 2 * (there // 2) + core

    x_next, x_prev = along_x(1), along_x(3)
    sibling = (w, n + 1 - 2 * core)
    barrier = pltpu.get_barrier_semaphore()

    def greet(device):
        pl.semaphore_signal(barrier, inc=1, device_id=device, device_id_type=MESH_ID)

    for device in (x_next, x_prev, (ahead, n), (behind, n), sibling):
        greet(device)
    for step in range(1, 4):
        greet((join_wide(x_lo, (y + step) % 4, z), n))
    for step in range(1, 16):
        greet((join_wide(x_lo, y, (z + step) % 16), n))
    at_home = core == x_lo
    targets = [(join_wide(core, y, z), k) for k in range(4)]
    sources = [(join_wide(k % 2, y, z), 2 * (k // 2) + x_lo) for k in range(4)]
    for device in targets + sources:

        @pl.when(jnp.logical_not(jnp.logical_and(device[0] == w, device[1] == n)))
        def _(device=device):
            greet(device)

    pl.semaphore_wait(barrier, 31 - 2 * at_home.astype(jnp.int32))

    def part(side, k):
        return pl.ds(pl.multiple_of(side * half_rows + k * rows, rows), rows)

    def send_own(k):
        for side, device in enumerate((x_next, x_prev)):
            at = part(side, k)
            pltpu.make_async_remote_copy(
                own.at[at], relay.at[at], own_sent, relay_in.at[side, k], device_id=device, device_id_type=MESH_ID
            ).start()

    def wait_for(ref, sem):
        pltpu.make_async_copy(ref, ref, sem).wait()

    def pass_on(k):
        for side, device in enumerate((x_next, x_prev)):
            at = part(side, k)
            wait_for(relay.at[at], relay_in.at[side, k])
            pltpu.make_async_remote_copy(
                relay.at[at], far.at[0, at], relay_sent, near_in.at[side, k], device_id=device, device_id_type=MESH_ID
            ).start()

    def send_near(k):
        for side in range(2):
            at = part(side, k)
            wait_for(far.at[0, at], near_in.at[side, k])
            pltpu.make_async_remote_copy(
                far.at[0, at], far.at[1, at], near_sent, next_in.at[side, k],
                device_id=(ahead, n), device_id_type=MESH_ID,
            ).start()

    def send_next(k):
        for side in range(2):
            at = part(side, k)
            wait_for(far.at[1, at], next_in.at[side, k])
            pltpu.make_async_remote_copy(
                far.at[1, at], far.at[2, at], next_sent, last_in, device_id=(ahead, n), device_id_type=MESH_ID
            ).start()

    send_own(0)
    send_own(1)
    partner = (n + 2) % 4
    column[...] = jnp.broadcast_to(vir[pl.ds(n, 1), :], (128, nvir)).T
    partner_row = vir[pl.ds(partner, 1), :]
    total[...] = jnp.zeros_like(total)
    dens[...] = jnp.zeros_like(dens)
    z_out[...] = jnp.zeros_like(z_out)

    def fill_table(s):
        there = (w + s) % 128
        for i in range(2):
            for j in range(2):
                level = occ[kpoint[n, w], i] + occ[kpoint[partner, there], j]
                alive = jnp.where(i < count[n, w], 1.0, 0.0) * jnp.where(j < count[partner, there], 1.0, 0.0)

                def some_rows(k, carry, i=i, j=j, level=level, alive=alive):
                    at = pl.multiple_of(k * 64, 64)
                    left = level - column[pl.ds(at, 64), :]
                    for c in range(nvir // 128):
                        gap = left - partner_row[:, c * 128 : (c + 1) * 128]
                        table[s, pl.ds(i * nvir + at, 64), j * nvir + c * 128 : j * nvir + (c + 1) * 128] = alive / gap
                    return carry

                lax.fori_loop(0, nvir // 64, some_rows, 0)

    def round_of(k, carry):
        pass_on(k)

        @pl.when(k < CHUNKS - 2)
        def _():
            send_own(k + 2)

        @pl.when(k >= 1)
        def _():
            send_near(k - 1)

        @pl.when(k < WINDOW)
        def _():
            fill_table(k)

        return carry

    lax.fori_loop(0, CHUNKS, round_of, 0)
    send_near(CHUNKS - 1)

    def last_round(k, carry):
        send_next(k)
        return carry

    lax.fori_loop(0, CHUNKS, last_round, 0)

    def add_gamma(s):
        for i in range(2):
            cols = slice(i * nvir, (i + 1) * nvir)
            total[:, cols] += lax.dot_general(
                far[s], mix[i], (((1,), (1,)), ((), ())), preferred_element_type=jnp.float32
            )

    def window_step(s, carry):
        @pl.when(s == WINDOW - 1)
        def _():
            wait_for(far.at[2], last_in)

        for i in range(2):
            left = own_t[i * nvir : (i + 1) * nvir, :]
            for j in range(2):
                cols = slice(j * nvir, (j + 1) * nvir)
                product = jnp.dot(left, far[s, :, cols], preferred_element_type=jnp.float32)
                amplitude = product * table[s, i * nvir : (i + 1) * nvir, cols]
                mixed = 2.0 * amplitude - amplitude.T
                amp[i, :, cols] = amplitude.astype(jnp.bfloat16)
                mix[i, :, cols] = mixed.astype(jnp.bfloat16)
            dens[...] += lax.dot_general(
                mix[i], amp[i], (((1,), (1,)), ((), ())), preferred_element_type=jnp.float32
            )

        @pl.when(s < WINDOW - 1)
        def _():
            add_gamma(s)

        return carry

    lax.fori_loop(0, WINDOW, window_step, 0)

    span = nvir // 2
    pltpu.make_async_remote_copy(
        dens.at[pl.ds(pl.multiple_of((1 - core) * span, span), span)], core_in, dsend.at[0], drecv.at[0],
        device_id=sibling, device_id_type=MESH_ID,
    ).start()
    add_gamma(WINDOW - 1)
    wait_for(core_in, drecv.at[0])
    kept = dens[pl.ds(pl.multiple_of(core * span, span), span), :] + core_in[...]
    y_out[...] = kept.reshape(y_out.shape)
    for step in range(1, 4):
        to = (y + step) % 4
        pltpu.make_async_remote_copy(
            y_out.at[to], y_in.at[step - 1], dsend.at[1], drecv.at[1],
            device_id=(join_wide(x_lo, to, z), n), device_id_type=MESH_ID,
        ).start()
    gamma[...] = total[...].astype(gamma.dtype)
    wait_for(y_in, drecv.at[1])
    z_sum[...] = y_out[y] + add_up(y_in, 3)
    for k in range(16):
        for r in range(3):
            for c in range(3):
                z_out[k, 3 * r + c : 3 * r + c + 1, :] = z_sum[3 * k + r : 3 * k + r + 1, c * 128 : (c + 1) * 128]
    for step in range(1, 16):
        to = (z + step) % 16
        pltpu.make_async_remote_copy(
            z_out.at[to], z_in.at[step - 1], dsend.at[2], drecv.at[2],
            device_id=(join_wide(x_lo, y, to), n), device_id_type=MESH_ID,
        ).start()
    wait_for(z_in, drecv.at[2])
    x_out[...] = z_out[z] + add_up(z_in, 15)
    for device in targets:
        here = jnp.logical_and(device[0] == w, device[1] == n)

        @pl.when(here)
        def _():
            pltpu.make_async_copy(x_out, x_in.at[x], drecv.at[3]).start()

        @pl.when(jnp.logical_not(here))
        def _(device=device):
            pltpu.make_async_remote_copy(
                x_out, x_in.at[x], dsend.at[3], drecv.at[3], device_id=device, device_id_type=MESH_ID
            ).start()

    wait_for(x_in, drecv.at[3])
    piece[...] = add_up(x_in, 4) * (1.0 / (4 * 128 * nvir))

    wait_for(own, own_sent)
    wait_for(own, relay_sent)
    wait_for(own, near_sent)
    wait_for(own, next_sent)
    wait_for(core_in, dsend.at[0])
    wait_for(y_in, dsend.at[1])
    wait_for(z_in, dsend.at[2])

    @pl.when(at_home)
    def _():
        wait_for(x_in.at[pl.ds(0, 3)], dsend.at[3])

    @pl.when(jnp.logical_not(at_home))
    def _():
        wait_for(x_in, dsend.at[3])


def pairs(own, own_t, vir, occ, kpoint, count):
    aux, width = own.shape
    nvir = vir.shape[1]
    bf16, f32 = jnp.bfloat16, jnp.float32
    dma = pltpu.SemaphoreType.DMA
    vmem = pl.BlockSpec(memory_space=pltpu.VMEM)
    smem = pl.BlockSpec(memory_space=pltpu.SMEM)
    return pl.pallas_call(
        pair_kernel,
        name="pairs",
        out_shape=(jax.ShapeDtypeStruct((aux, width), bf16), jax.ShapeDtypeStruct((16, 128), f32)),
        in_specs=[vmem, vmem, vmem, smem, smem, smem],
        out_specs=(vmem, vmem),
        scratch_shapes=[
            pltpu.VMEM((aux, width), bf16),
            pltpu.VMEM((WINDOW, aux, width), bf16),
            pltpu.VMEM((WINDOW, width, width), f32),
            pltpu.VMEM((nvir, 128), f32),
            pltpu.VMEM((aux, width), f32),
            pltpu.VMEM((nvir, nvir), f32),
            pltpu.VMEM((2, nvir, width), bf16),
            pltpu.VMEM((2, nvir, width), bf16),
            pltpu.VMEM((nvir // 2, nvir), f32),
            pltpu.VMEM((4, nvir // 8, nvir), f32),
            pltpu.VMEM((3, nvir // 8, nvir), f32),
            pltpu.VMEM((nvir // 8, nvir), f32),
            pltpu.VMEM((16, 16, 128), f32),
            pltpu.VMEM((15, 16, 128), f32),
            pltpu.VMEM((16, 128), f32),
            pltpu.VMEM((4, 16, 128), f32),
            dma,
            dma((2, CHUNKS)),
            dma,
            dma((2, CHUNKS)),
            dma,
            dma((2, CHUNKS)),
            dma,
            dma,
            dma((4,)),
            dma((4,)),
        ],
        compiler_params=pltpu.CompilerParams(
            collective_id=1, has_side_effects=True, vmem_limit_bytes=60000 * 1024
        ),
    )(own, own_t, vir, occ, kpoint, count)


def shards(raw_ints, metric_root, occ_energy, vir_energy, block_kpoint, occ_count):
    nvir = raw_ints.shape[4]
    blocks, roots = regroup(raw_ints, metric_root)
    aux = metric_root.shape[1]
    blocks = blocks.reshape(aux, 2 * nvir)
    roots = roots.reshape(aux, aux)
    over = (((0,), (0,)), ((), ()))
    own = lax.dot_general(roots, blocks, over, preferred_element_type=jnp.float32).astype(jnp.bfloat16)
    own_t = lax.dot_general(blocks, roots, over, preferred_element_type=jnp.float32).astype(jnp.bfloat16)
    gamma, piece = pairs(own, own_t, vir_energy, occ_energy, block_kpoint, occ_count)
    share = 3 * nvir // 4
    density = lax.dynamic_slice(piece.reshape(-1), (lax.axis_index("narrow") * share,), (share,))
    return gamma.reshape(1, aux, 1, 2, nvir), density


def solution(mesh):
    placed = (P("narrow", "wide", None, None, None), P("wide", None), P(), P(), P(), P())
    return jax.shard_map(
        shards,
        mesh=mesh,
        in_specs=placed,
        out_specs=(P("narrow", None, "wide", None, None), P(("wide", "narrow"))),
        check_vma=False,
    )
```

```python
import functools

import jax
import jax.numpy as jnp
from jax import lax
from jax.experimental import pallas as pl
from jax.experimental.pallas import tpu as pltpu

from jax.sharding import PartitionSpec as P

MESH_ID = pl.DeviceIdType.MESH


def split_wide(w):
    return w // 64, (w // 16) % 4, w % 16


def join_wide(x, y, z):
    return x * 64 + y * 16 + z


def slot_of(w):
    x, y, z = split_wide(w)
    return x * 64 + y * 16 + (z % 2) * 8 + z // 2


def peer_at(step, w):
    x, y, z = split_wide(w)
    turn, side = step // 8, step % 8
    half = (turn + 1) // 2
    dz = jnp.where(turn % 2 == 1, half, 16 - half)
    return join_wide((x + side // 4) % 2, (y + side % 4) % 4, (z + dz) % 16)


def regroup_kernel(raw, root, recv, metric, ssem, rsem, msend, mrecv):
    w = lax.axis_index("wide")
    n = lax.axis_index("narrow")
    core = n % 2
    sibling = n + 1 - 2 * core
    x, y, z = split_wide(w)
    barrier = pltpu.get_barrier_semaphore()

    def greet(step, carry):
        pl.semaphore_signal(barrier, inc=1, device_id=((w + step) % 128, n), device_id_type=MESH_ID)
        return carry

    lax.fori_loop(1, 128, greet, 0)
    pl.semaphore_signal(barrier, inc=1, device_id=(w, sibling), device_id_type=MESH_ID)
    pl.semaphore_wait(barrier, 128)

    mine = slot_of(w)
    par = (z + core) % 2

    def send_metric(step, carry):
        dz = 2 * step + core

        @pl.when(dz != 0)
        def _():
            pltpu.make_async_remote_copy(
                root, metric.at[mine], msend.at[0], mrecv.at[0],
                device_id=(join_wide(x, y, (z + dz) % 16), n), device_id_type=MESH_ID,
            ).start()

        @pl.when(dz == 0)
        def _():
            pltpu.make_async_copy(root, metric.at[mine], mrecv.at[0]).start()

        return carry

    lax.fori_loop(0, 8, send_metric, 0)
    pltpu.make_async_copy(raw.at[0, :, w], recv.at[mine], rsem).start()

    def send_raw(step, carry):
        peer = peer_at(step, w)

        @pl.when(peer != w)
        def _():
            pltpu.make_async_remote_copy(
                raw.at[0, :, peer], recv.at[mine], ssem, rsem, device_id=(peer, n), device_id_type=MESH_ID
            ).start()

        return carry

    lax.fori_loop(0, 128, send_raw, 0)

    line = metric.at[pl.ds(pl.multiple_of(x * 64 + y * 16 + par * 8, 8), 8)]
    pltpu.make_async_copy(line, line, mrecv.at[0]).wait()
    for step in range(1, 4):
        pltpu.make_async_remote_copy(
            line, line, msend.at[1], mrecv.at[1],
            device_id=(join_wide(x, (y + step) % 4, z), n), device_id_type=MESH_ID,
        ).start()
    three = metric.at[pl.ds(0, 24)]
    pltpu.make_async_copy(three, three, mrecv.at[1]).wait()
    copies = []
    for row in range(4):
        part = metric.at[pl.ds(pl.multiple_of(x * 64 + row * 16 + par * 8, 8), 8)]
        copies.append(pltpu.make_async_remote_copy(
            part, part, msend.at[2], mrecv.at[2],
            device_id=(join_wide(1 - x, y, z), n), device_id_type=MESH_ID,
        ))
    for copy in copies:
        copy.start()
    four = metric.at[pl.ds(0, 32)]
    pltpu.make_async_copy(four, four, mrecv.at[2]).wait()
    for row in range(8):
        part = metric.at[pl.ds(pl.multiple_of(row * 16 + par * 8, 8), 8)]
        pltpu.make_async_remote_copy(
            part, part, msend.at[3], mrecv.at[3], device_id=(w, sibling), device_id_type=MESH_ID
        ).start()
    eight = metric.at[pl.ds(0, 64)]
    pltpu.make_async_copy(eight, eight, mrecv.at[3]).wait()

    @pl.when(core == 0)
    def _():
        part = metric.at[pl.ds(0, 7)]
        pltpu.make_async_copy(part, part, msend.at[0]).wait()

    @pl.when(core == 1)
    def _():
        part = metric.at[pl.ds(0, 8)]
        pltpu.make_async_copy(part, part, msend.at[0]).wait()

    pltpu.make_async_copy(three, three, msend.at[1]).wait()
    pltpu.make_async_copy(four, four, msend.at[2]).wait()
    pltpu.make_async_copy(eight, eight, msend.at[3]).wait()
    others = recv.at[pl.ds(0, 127)]
    pltpu.make_async_copy(others, others, ssem).wait()
    pltpu.make_async_copy(recv, recv, rsem).wait()


def regroup(raw_ints, metric_root):
    rows, cols = metric_root.shape
    return pl.pallas_call(
        regroup_kernel,
        name="regroup",
        out_shape=(
            jax.ShapeDtypeStruct((128,) + raw_ints.shape[1:2] + raw_ints.shape[3:], jnp.bfloat16),
            jax.ShapeDtypeStruct((128, rows, cols), jnp.bfloat16),
        ),
        in_specs=[pl.BlockSpec(memory_space=pltpu.VMEM)] * 2,
        out_specs=(pl.BlockSpec(memory_space=pltpu.VMEM),) * 2,
        scratch_shapes=[
            pltpu.SemaphoreType.DMA,
            pltpu.SemaphoreType.DMA,
            pltpu.SemaphoreType.DMA((4,)),
            pltpu.SemaphoreType.DMA((4,)),
        ],
        compiler_params=pltpu.CompilerParams(collective_id=0, has_side_effects=True),
    )(raw_ints, metric_root)


CHUNKS = 5
WINDOW = 3


def add_up(ref, count):
    total = ref[0]
    for k in range(1, count):
        total = total + ref[k]
    return total


def pair_kernel(
    own, vir, occ, kpoint, count,
    gamma, piece,
    own_t, relay, transit, far, table, column, total, dens, amp, mix,
    core_in, y_out, y_in, z_sum, z_out, z_in, x_out, x_in,
    own_sent, relay_in, relay_sent, near_in, near_sent, next_in, next_sent, last_in, turn_in, turn_sent, core_got, dsend, drecv,
):
    aux, width = own.shape
    nvir = vir.shape[1]
    half_rows = aux // 2
    rows = half_rows // CHUNKS
    w = lax.axis_index("wide")
    n = lax.axis_index("narrow")
    core, x_hi = n % 2, n // 2
    x_lo, y, z = split_wide(w)
    x = 2 * x_hi + x_lo
    ahead, behind = (w + 127) % 128, (w + 1) % 128

    def along_x(step):
        there = (x + step) % 4
        return join_wide(there % 2, y, z), 2 * (there // 2) + core

    x_next, x_prev = along_x(1), along_x(3)
    sibling = (w, n + 1 - 2 * core)
    barrier = pltpu.get_barrier_semaphore()

    def greet(device):
        pl.semaphore_signal(barrier, inc=1, device_id=device, device_id_type=MESH_ID)

    for device in (x_next, x_prev, (ahead, n), (behind, n), sibling):
        greet(device)
    for step in range(1, 4):
        greet((join_wide(x_lo, (y + step) % 4, z), n))
    for step in range(1, 16):
        greet((join_wide(x_lo, y, (z + step) % 16), n))
    at_home = core == x_lo
    targets = [(join_wide(core, y, z), k) for k in range(4)]
    sources = [(join_wide(k % 2, y, z), 2 * (k // 2) + x_lo) for k in range(4)]
    for device in targets + sources:

        @pl.when(jnp.logical_not(jnp.logical_and(device[0] == w, device[1] == n)))
        def _(device=device):
            greet(device)

    corner = jnp.logical_and(y == 0, z == 0)
    corner_end = jnp.logical_and(y == 3, z == 15)
    turned = join_wide(1 - x_lo, y, z)

    @pl.when(corner)
    def _():
        greet((turned, n))
        greet((join_wide(x_lo, 3, 15), n))

    @pl.when(corner_end)
    def _():
        greet((join_wide(x_lo, 0, 0), n))

    extra = 2 * corner.astype(jnp.int32) + corner_end.astype(jnp.int32)
    pl.semaphore_wait(barrier, 31 - 2 * at_home.astype(jnp.int32) + extra)

    def part(side, k):
        return pl.ds(pl.multiple_of(side * half_rows + k * rows, rows), rows)

    def send_own(k):
        for side, device in enumerate((x_next, x_prev)):
            at = part(side, k)
            pltpu.make_async_remote_copy(
                own.at[at], relay.at[at], own_sent, relay_in.at[side, k], device_id=device, device_id_type=MESH_ID
            ).start()

    def wait_for(ref, sem):
        pltpu.make_async_copy(ref, ref, sem).wait()

    def pass_on(k):
        for side, device in enumerate((x_next, x_prev)):
            at = part(side, k)
            wait_for(relay.at[at], relay_in.at[side, k])
            pltpu.make_async_remote_copy(
                relay.at[at], far.at[0, at], relay_sent, near_in.at[side, k], device_id=device, device_id_type=MESH_ID
            ).start()

    def send_near(k):
        for side in range(2):
            at = part(side, k)
            wait_for(far.at[0, at], near_in.at[side, k])
            pltpu.make_async_remote_copy(
                far.at[0, at], far.at[1, at], near_sent, next_in.at[side, k],
                device_id=(ahead, n), device_id_type=MESH_ID,
            ).start()

    def send_next(k):
        for side in range(2):
            at = part(side, k)
            wait_for(far.at[1, at], next_in.at[side, k])

            @pl.when(corner)
            def _(side=side, at=at):
                pltpu.make_async_remote_copy(
                    far.at[1, at], transit.at[at], next_sent, turn_in.at[side, k],
                    device_id=(turned, n), device_id_type=MESH_ID,
                ).start()

            @pl.when(jnp.logical_not(corner))
            def _(at=at):
                pltpu.make_async_remote_copy(
                    far.at[1, at], far.at[2, at], next_sent, last_in, device_id=(ahead, n), device_id_type=MESH_ID
                ).start()

    def send_turned(k):
        for side in range(2):
            at = part(side, k)
            wait_for(transit.at[at], turn_in.at[side, k])
            pltpu.make_async_remote_copy(
                transit.at[at], far.at[2, at], turn_sent, last_in,
                device_id=(join_wide(x_lo, 3, 15), n), device_id_type=MESH_ID,
            ).start()

    send_own(0)
    send_own(1)
    partner = (n + 2) % 4
    own_t[...] = own[...].T
    column[...] = jnp.broadcast_to(vir[pl.ds(n, 1), :], (128, nvir)).T
    partner_row = vir[pl.ds(partner, 1), :]
    total[...] = jnp.zeros_like(total)
    dens[...] = jnp.zeros_like(dens)

    def fill_table(s):
        there = (w + s) % 128
        for i in range(2):
            for j in range(2):
                level = occ[kpoint[n, w], i] + occ[kpoint[partner, there], j]
                alive = jnp.where(i < count[n, w], 1.0, 0.0) * jnp.where(j < count[partner, there], 1.0, 0.0)

                def some_rows(k, carry, i=i, j=j, level=level, alive=alive):
                    at = pl.multiple_of(k * 64, 64)
                    left = level - column[pl.ds(at, 64), :]
                    for c in range(nvir // 128):
                        gap = left - partner_row[:, c * 128 : (c + 1) * 128]
                        table[s, pl.ds(i * nvir + at, 64), j * nvir + c * 128 : j * nvir + (c + 1) * 128] = alive / gap
                    return carry

                lax.fori_loop(0, nvir // 64, some_rows, 0)

    def round_of(k, carry):
        pass_on(k)

        @pl.when(k < CHUNKS - 2)
        def _():
            send_own(k + 2)

        @pl.when(k >= 1)
        def _():
            send_near(k - 1)

        @pl.when(k < WINDOW)
        def _():
            fill_table(k)

        return carry

    lax.fori_loop(0, CHUNKS, round_of, 0)
    send_near(CHUNKS - 1)

    def last_round(k, carry):
        send_next(k)

        @pl.when(corner)
        def _():
            send_turned(k)

        return carry

    lax.fori_loop(0, CHUNKS, last_round, 0)

    def add_gamma(s):
        for i in range(2):
            cols = slice(i * nvir, (i + 1) * nvir)
            total[:, cols] += lax.dot_general(
                far[s], mix[i], (((1,), (1,)), ((), ())), preferred_element_type=jnp.float32
            )

    def window_step(s, carry):
        @pl.when(s == WINDOW - 1)
        def _():
            wait_for(far.at[2], last_in)

        for i in range(2):
            left = own_t[i * nvir : (i + 1) * nvir, :]
            for j in range(2):
                cols = slice(j * nvir, (j + 1) * nvir)
                product = jnp.dot(left, far[s, :, cols], preferred_element_type=jnp.float32)
                amplitude = product * table[s, i * nvir : (i + 1) * nvir, cols]
                mixed = 2.0 * amplitude - amplitude.T
                amp[i, :, cols] = amplitude.astype(jnp.bfloat16)
                mix[i, :, cols] = mixed.astype(jnp.bfloat16)
            dens[...] += lax.dot_general(
                mix[i], amp[i], (((1,), (1,)), ((), ())), preferred_element_type=jnp.float32
            )

        @pl.when(s < WINDOW - 1)
        def _():
            add_gamma(s)

        return carry

    lax.fori_loop(0, WINDOW, window_step, 0)

    span = nvir // 8

    def share(of_core, row):
        return dens.at[pl.ds(pl.multiple_of(of_core * 4 * span + row * span, span), span)]

    order = [(y + step) % 4 for step in (2, 1, 3, 0)]
    for row in order:
        pltpu.make_async_remote_copy(
            share(1 - core, row), core_in.at[row], dsend.at[0], core_got.at[row],
            device_id=sibling, device_id_type=MESH_ID,
        ).start()
    for step, row in zip((2, 1, 3), order):
        wait_for(core_in.at[row], core_got.at[row])
        y_out[row] = share(core, row)[...] + core_in[row]
        pltpu.make_async_remote_copy(
            y_out.at[row], y_in.at[step - 1], dsend.at[1], drecv.at[1],
            device_id=(join_wide(x_lo, row, z), n), device_id_type=MESH_ID,
        ).start()
    add_gamma(WINDOW - 1)
    wait_for(core_in.at[y], core_got.at[y])
    mine = share(core, y)[...] + core_in[y]
    wait_for(y_in, drecv.at[1])
    z_sum[...] = mine + add_up(y_in, 3)
    for k in range(16):
        for r in range(3):
            for c in range(3):
                z_out[k, 3 * r + c : 3 * r + c + 1, :] = z_sum[3 * k + r : 3 * k + r + 1, c * 128 : (c + 1) * 128]
    for step in range(1, 16):
        to = (z + step) % 16
        pltpu.make_async_remote_copy(
            z_out.at[to], z_in.at[step - 1], dsend.at[2], drecv.at[2],
            device_id=(join_wide(x_lo, y, to), n), device_id_type=MESH_ID,
        ).start()
    gamma[...] = total[...].astype(gamma.dtype)
    wait_for(z_in, drecv.at[2])
    x_out[...] = z_out[z] + add_up(z_in, 15)
    for device in targets:
        here = jnp.logical_and(device[0] == w, device[1] == n)

        @pl.when(here)
        def _():
            pltpu.make_async_copy(x_out, x_in.at[x], drecv.at[3]).start()

        @pl.when(jnp.logical_not(here))
        def _(device=device):
            pltpu.make_async_remote_copy(
                x_out, x_in.at[x], dsend.at[3], drecv.at[3], device_id=device, device_id_type=MESH_ID
            ).start()

    wait_for(x_in, drecv.at[3])
    piece[...] = add_up(x_in, 4) * (1.0 / (4 * 128 * nvir))

    wait_for(own, own_sent)
    wait_for(own, relay_sent)
    wait_for(own, near_sent)
    wait_for(own, next_sent)

    @pl.when(corner)
    def _():
        wait_for(transit, turn_sent)

    wait_for(core_in, dsend.at[0])
    wait_for(y_in, dsend.at[1])
    wait_for(z_in, dsend.at[2])

    @pl.when(at_home)
    def _():
        wait_for(x_in.at[pl.ds(0, 3)], dsend.at[3])

    @pl.when(jnp.logical_not(at_home))
    def _():
        wait_for(x_in, dsend.at[3])


def pairs(own, vir, occ, kpoint, count):
    aux, width = own.shape
    nvir = vir.shape[1]
    bf16, f32 = jnp.bfloat16, jnp.float32
    dma = pltpu.SemaphoreType.DMA
    vmem = pl.BlockSpec(memory_space=pltpu.VMEM)
    smem = pl.BlockSpec(memory_space=pltpu.SMEM)
    return pl.pallas_call(
        pair_kernel,
        name="pairs",
        out_shape=(jax.ShapeDtypeStruct((aux, width), bf16), jax.ShapeDtypeStruct((9, 128), f32)),
        in_specs=[vmem, vmem, smem, smem, smem],
        out_specs=(vmem, vmem),
        scratch_shapes=[
            pltpu.VMEM((width, aux), bf16),
            pltpu.VMEM((aux, width), bf16),
            pltpu.VMEM((aux, width), bf16),
            pltpu.VMEM((WINDOW, aux, width), bf16),
            pltpu.VMEM((WINDOW, width, width), f32),
            pltpu.VMEM((nvir, 128), f32),
            pltpu.VMEM((aux, width), f32),
            pltpu.VMEM((nvir, nvir), f32),
            pltpu.VMEM((2, nvir, width), bf16),
            pltpu.VMEM((2, nvir, width), bf16),
            pltpu.VMEM((4, nvir // 8, nvir), f32),
            pltpu.VMEM((4, nvir // 8, nvir), f32),
            pltpu.VMEM((3, nvir // 8, nvir), f32),
            pltpu.VMEM((nvir // 8, nvir), f32),
            pltpu.VMEM((16, 9, 128), f32),
            pltpu.VMEM((15, 9, 128), f32),
            pltpu.VMEM((9, 128), f32),
            pltpu.VMEM((4, 9, 128), f32),
            dma,
            dma((2, CHUNKS)),
            dma,
            dma((2, CHUNKS)),
            dma,
            dma((2, CHUNKS)),
            dma,
            dma,
            dma((2, CHUNKS)),
            dma,
            dma((4,)),
            dma((4,)),
            dma((4,)),
        ],
        compiler_params=pltpu.CompilerParams(
            collective_id=1, has_side_effects=True, vmem_limit_bytes=60000 * 1024
        ),
    )(own, vir, occ, kpoint, count)


def shards(raw_ints, metric_root, occ_energy, vir_energy, block_kpoint, occ_count):
    nvir = raw_ints.shape[4]
    blocks, roots = regroup(raw_ints, metric_root)
    aux = metric_root.shape[1]
    blocks = blocks.reshape(aux, 2 * nvir)
    roots = roots.reshape(aux, aux)
    over = (((0,), (0,)), ((), ()))
    own = lax.dot_general(roots, blocks, over, preferred_element_type=jnp.float32).astype(jnp.bfloat16)
    gamma, piece = pairs(own, vir_energy, occ_energy, block_kpoint, occ_count)
    share = 3 * nvir // 4
    density = lax.dynamic_slice(piece.reshape(-1), (lax.axis_index("narrow") * share,), (share,))
    return gamma.reshape(1, aux, 1, 2, nvir), density


def solution(mesh):
    placed = (P("narrow", "wide", None, None, None), P("wide", None), P(), P(), P(), P())
    return jax.shard_map(
        shards,
        mesh=mesh,
        in_specs=placed,
        out_specs=(P("narrow", None, "wide", None, None), P(("wide", "narrow"))),
        check_vma=False,
    )
```

```python
import functools

import jax
import jax.numpy as jnp
from jax import lax
from jax.experimental import pallas as pl
from jax.experimental.pallas import tpu as pltpu

from jax.sharding import PartitionSpec as P

MESH_ID = pl.DeviceIdType.MESH


def split_wide(w):
    return w // 64, (w // 16) % 4, w % 16


def join_wide(x, y, z):
    return x * 64 + y * 16 + z


def slot_of(w):
    x, y, z = split_wide(w)
    return x * 64 + y * 16 + (z % 2) * 8 + z // 2


def peer_at(step, w):
    x, y, z = split_wide(w)
    turn, side = step // 8, step % 8
    half = (turn + 1) // 2
    dz = jnp.where(turn % 2 == 1, half, 16 - half)
    return join_wide((x + side // 4) % 2, (y + side % 4) % 4, (z + dz) % 16)


CHUNKS = 5
WINDOW = 3


def add_up(ref, count):
    total = ref[0]
    for k in range(1, count):
        total = total + ref[k]
    return total


def window_kernel(
    raw, root, vir, occ, kpoint, count,
    gamma, piece,
    recv, metric, root_t, rows_in, own, own_t, relay, transit, far, table, column, total, dens, amp, mix,
    core_in, y_out, y_in, z_sum, z_out, z_in, x_out, x_in,
    own_sent, relay_in, relay_sent, near_in, near_sent, next_in, next_sent, last_in, turn_in, turn_sent, core_got, dsend, drecv, ssem, rsem, msend, mrecv,
):
    aux, width = own.shape
    nvir = vir.shape[1]
    half_rows = aux // 2
    rows = half_rows // CHUNKS
    w = lax.axis_index("wide")
    n = lax.axis_index("narrow")
    core, x_hi = n % 2, n // 2
    x_lo, y, z = split_wide(w)
    x = 2 * x_hi + x_lo
    ahead, behind = (w + 127) % 128, (w + 1) % 128

    def along_x(step):
        there = (x + step) % 4
        return join_wide(there % 2, y, z), 2 * (there // 2) + core

    x_next, x_prev = along_x(1), along_x(3)
    sibling = (w, n + 1 - 2 * core)
    barrier = pltpu.get_barrier_semaphore()

    def greet(device):
        pl.semaphore_signal(barrier, inc=1, device_id=device, device_id_type=MESH_ID)

    def greet_wide(step, carry):
        greet(((w + step) % 128, n))
        return carry

    lax.fori_loop(1, 128, greet_wide, 0)
    for device in (x_next, x_prev, sibling):
        greet(device)
    at_home = core == x_lo
    targets = [(join_wide(core, y, z), k) for k in range(4)]
    sources = [(join_wide(k % 2, y, z), 2 * (k // 2) + x_lo) for k in range(4)]
    for device in targets + sources:

        @pl.when(jnp.logical_not(jnp.logical_and(device[0] == w, device[1] == n)))
        def _(device=device):
            greet(device)

    corner = jnp.logical_and(y == 0, z == 0)
    turned = join_wide(1 - x_lo, y, z)

    pl.semaphore_wait(barrier, 138 - 2 * at_home.astype(jnp.int32))

    slot = slot_of(w)
    par = (z + core) % 2

    def send_metric(step, carry):
        dz = 2 * step + core

        @pl.when(dz != 0)
        def _():
            pltpu.make_async_remote_copy(
                root, metric.at[slot], msend.at[0], mrecv.at[0],
                device_id=(join_wide(x_lo, y, (z + dz) % 16), n), device_id_type=MESH_ID,
            ).start()

        @pl.when(dz == 0)
        def _():
            pltpu.make_async_copy(root, metric.at[slot], mrecv.at[0]).start()

        return carry

    lax.fori_loop(0, 8, send_metric, 0)
    pltpu.make_async_copy(raw.at[0, :, w], recv.at[slot], rsem).start()

    def send_raw(step, carry):
        peer = peer_at(step, w)

        @pl.when(peer != w)
        def _():
            pltpu.make_async_remote_copy(
                raw.at[0, :, peer], recv.at[slot], ssem, rsem, device_id=(peer, n), device_id_type=MESH_ID
            ).start()

        return carry

    lax.fori_loop(0, 128, send_raw, 0)

    def part(side, k):
        return pl.ds(pl.multiple_of(side * half_rows + k * rows, rows), rows)

    def send_own(k):
        for side, device in enumerate((x_next, x_prev)):
            at = part(side, k)
            pltpu.make_async_remote_copy(
                own.at[at], relay.at[at], own_sent, relay_in.at[side, k], device_id=device, device_id_type=MESH_ID
            ).start()

    def wait_for(ref, sem):
        pltpu.make_async_copy(ref, ref, sem).wait()

    def pass_on(k):
        for side, device in enumerate((x_next, x_prev)):
            at = part(side, k)
            wait_for(relay.at[at], relay_in.at[side, k])
            pltpu.make_async_remote_copy(
                relay.at[at], far.at[0, at], relay_sent, near_in.at[side, k], device_id=device, device_id_type=MESH_ID
            ).start()

            @pl.when(jnp.logical_and(corner, x_lo == side))
            def _(side=side, at=at):
                pltpu.make_async_remote_copy(
                    relay.at[at], far.at[1, at], near_sent, next_in.at[side, k],
                    device_id=(join_wide(x_lo, 3, 15), n), device_id_type=MESH_ID,
                ).start()

    def send_near(k):
        for side in range(2):
            at = part(side, k)
            wait_for(far.at[0, at], near_in.at[side, k])

            @pl.when(jnp.logical_or(jnp.logical_not(corner), x_lo == side))
            def _(side=side, at=at):
                pltpu.make_async_remote_copy(
                    far.at[0, at], far.at[1, at], near_sent, next_in.at[side, k],
                    device_id=(ahead, n), device_id_type=MESH_ID,
                ).start()

    def send_next(k):
        for side in range(2):
            at = part(side, k)
            wait_for(far.at[1, at], next_in.at[side, k])

            @pl.when(corner)
            def _(side=side, at=at):
                pltpu.make_async_remote_copy(
                    far.at[1, at], transit.at[at], next_sent, turn_in.at[side, k],
                    device_id=(turned, n), device_id_type=MESH_ID,
                ).start()

            @pl.when(jnp.logical_not(corner))
            def _(at=at):
                pltpu.make_async_remote_copy(
                    far.at[1, at], far.at[2, at], next_sent, last_in, device_id=(ahead, n), device_id_type=MESH_ID
                ).start()

    def send_turned(k):
        for side in range(2):
            at = part(side, k)
            wait_for(transit.at[at], turn_in.at[side, k])
            pltpu.make_async_remote_copy(
                transit.at[at], far.at[2, at], turn_sent, last_in,
                device_id=(join_wide(x_lo, 3, 15), n), device_id_type=MESH_ID,
            ).start()

    line = metric.at[pl.ds(pl.multiple_of(x_lo * 64 + y * 16 + par * 8, 8), 8)]
    pltpu.make_async_copy(line, line, mrecv.at[0]).wait()
    for step in range(1, 4):
        pltpu.make_async_remote_copy(
            line, line, msend.at[1], mrecv.at[1],
            device_id=(join_wide(x_lo, (y + step) % 4, z), n), device_id_type=MESH_ID,
        ).start()
    three = metric.at[pl.ds(0, 24)]
    pltpu.make_async_copy(three, three, mrecv.at[1]).wait()
    copies = []
    for row in range(4):
        span_ref = metric.at[pl.ds(pl.multiple_of(x_lo * 64 + row * 16 + par * 8, 8), 8)]
        copies.append(pltpu.make_async_remote_copy(
            span_ref, span_ref, msend.at[2], mrecv.at[2],
            device_id=(join_wide(1 - x_lo, y, z), n), device_id_type=MESH_ID,
        ))
    for copy in copies:
        copy.start()
    four = metric.at[pl.ds(0, 32)]
    pltpu.make_async_copy(four, four, mrecv.at[2]).wait()
    for row in range(8):
        span_ref = metric.at[pl.ds(pl.multiple_of(row * 16 + par * 8, 8), 8)]
        pltpu.make_async_remote_copy(
            span_ref, span_ref, msend.at[3], mrecv.at[3], device_id=sibling, device_id_type=MESH_ID
        ).start()
    eight = metric.at[pl.ds(0, 64)]
    pltpu.make_async_copy(eight, eight, mrecv.at[3]).wait()

    partner = (n + 2) % 4
    column[...] = jnp.broadcast_to(vir[pl.ds(n, 1), :], (128, nvir)).T
    partner_row = vir[pl.ds(partner, 1), :]
    total[...] = jnp.zeros_like(total)
    dens[...] = jnp.zeros_like(dens)
    for q in range(5):
        root_t[:, q * 128 : (q + 1) * 128] = metric[:, q, :].T

    def fill_table(s):
        there = (w + s) % 128
        for i in range(2):
            for j in range(2):
                level = occ[kpoint[n, w], i] + occ[kpoint[partner, there], j]
                alive = jnp.where(i < count[n, w], 1.0, 0.0) * jnp.where(j < count[partner, there], 1.0, 0.0)

                def some_rows(k, carry, i=i, j=j, level=level, alive=alive):
                    at = pl.multiple_of(k * 64, 64)
                    left = level - column[pl.ds(at, 64), :]
                    for c in range(nvir // 128):
                        gap = left - partner_row[:, c * 128 : (c + 1) * 128]
                        table[s, pl.ds(i * nvir + at, 64), j * nvir + c * 128 : j * nvir + (c + 1) * 128] = alive / gap
                    return carry

                lax.fori_loop(0, nvir // 64, some_rows, 0)

    def table_of(k, carry):
        fill_table(k)
        return carry

    lax.fori_loop(0, WINDOW, table_of, 0)
    pltpu.make_async_copy(recv, recv, rsem).wait()
    for q in range(5):
        for o in range(2):
            rows_in[q * 128 : (q + 1) * 128, o * nvir : (o + 1) * nvir] = recv[:, q, o, :]

    def fit(k, carry):
        for side in range(2):
            at = part(side, k)
            own[at, :] = jnp.dot(root_t[at, :], rows_in[...], preferred_element_type=jnp.float32).astype(own.dtype)
        return carry

    lax.fori_loop(0, CHUNKS, fit, 0)
    send_own(0)
    send_own(1)
    own_t[...] = own[...].T

    def round_of(k, carry):
        pass_on(k)

        @pl.when(k < CHUNKS - 2)
        def _():
            send_own(k + 2)

        @pl.when(k >= 1)
        def _():
            send_near(k - 1)

        return carry

    lax.fori_loop(0, CHUNKS, round_of, 0)
    send_near(CHUNKS - 1)

    def last_round(k, carry):
        send_next(k)

        @pl.when(corner)
        def _():
            send_turned(k)

        return carry

    lax.fori_loop(0, CHUNKS, last_round, 0)

    def add_gamma(s):
        for i in range(2):
            cols = slice(i * nvir, (i + 1) * nvir)
            total[:, cols] += lax.dot_general(
                far[s], mix[i], (((1,), (1,)), ((), ())), preferred_element_type=jnp.float32
            )

    def window_step(s, carry):
        @pl.when(s == WINDOW - 1)
        def _():
            wait_for(far.at[2], last_in)

        for i in range(2):
            left = own_t[i * nvir : (i + 1) * nvir, :]
            for j in range(2):
                cols = slice(j * nvir, (j + 1) * nvir)
                product = jnp.dot(left, far[s, :, cols], preferred_element_type=jnp.float32)
                amplitude = product * table[s, i * nvir : (i + 1) * nvir, cols]
                mixed = 2.0 * amplitude - amplitude.T
                amp[i, :, cols] = amplitude.astype(jnp.bfloat16)
                mix[i, :, cols] = mixed.astype(jnp.bfloat16)
            dens[...] += lax.dot_general(
                mix[i], amp[i], (((1,), (1,)), ((), ())), preferred_element_type=jnp.float32
            )

        @pl.when(s < WINDOW - 1)
        def _():
            add_gamma(s)

        return carry

    lax.fori_loop(0, WINDOW, window_step, 0)

    span = nvir // 8

    def share(of_core, row):
        return dens.at[pl.ds(pl.multiple_of(of_core * 4 * span + row * span, span), span)]

    order = [(y + step) % 4 for step in (2, 1, 3, 0)]
    for row in order:
        pltpu.make_async_remote_copy(
            share(1 - core, row), core_in.at[row], dsend.at[0], core_got.at[row],
            device_id=sibling, device_id_type=MESH_ID,
        ).start()
    for step, row in zip((2, 1, 3), order):
        wait_for(core_in.at[row], core_got.at[row])
        y_out[row] = share(core, row)[...] + core_in[row]
        pltpu.make_async_remote_copy(
            y_out.at[row], y_in.at[step - 1], dsend.at[1], drecv.at[1],
            device_id=(join_wide(x_lo, row, z), n), device_id_type=MESH_ID,
        ).start()
    add_gamma(WINDOW - 1)
    wait_for(core_in.at[y], core_got.at[y])
    mine = share(core, y)[...] + core_in[y]
    wait_for(y_in, drecv.at[1])
    z_sum[...] = mine + add_up(y_in, 3)
    for k in range(16):
        for r in range(3):
            for c in range(3):
                z_out[k, 3 * r + c : 3 * r + c + 1, :] = z_sum[3 * k + r : 3 * k + r + 1, c * 128 : (c + 1) * 128]
    for step in range(1, 16):
        to = (z + step) % 16
        pltpu.make_async_remote_copy(
            z_out.at[to], z_in.at[step - 1], dsend.at[2], drecv.at[2],
            device_id=(join_wide(x_lo, y, to), n), device_id_type=MESH_ID,
        ).start()
    for i in range(2):
        gamma[:, i, :] = total[:, i * nvir : (i + 1) * nvir].astype(gamma.dtype)
    wait_for(z_in, drecv.at[2])
    x_out[...] = z_out[z] + add_up(z_in, 15)
    for device in targets:
        here = jnp.logical_and(device[0] == w, device[1] == n)

        @pl.when(here)
        def _():
            pltpu.make_async_copy(x_out, x_in.at[x], drecv.at[3]).start()

        @pl.when(jnp.logical_not(here))
        def _(device=device):
            pltpu.make_async_remote_copy(
                x_out, x_in.at[x], dsend.at[3], drecv.at[3], device_id=device, device_id_type=MESH_ID
            ).start()

    wait_for(x_in, drecv.at[3])
    piece[...] = add_up(x_in, 4) * (1.0 / (4 * 128 * nvir))

    wait_for(own, own_sent)
    wait_for(own, relay_sent)
    wait_for(own, near_sent)
    wait_for(own, next_sent)

    @pl.when(corner)
    def _():
        wait_for(transit, turn_sent)

    wait_for(core_in, dsend.at[0])
    wait_for(y_in, dsend.at[1])
    wait_for(z_in, dsend.at[2])

    @pl.when(at_home)
    def _():
        wait_for(x_in.at[pl.ds(0, 3)], dsend.at[3])

    @pl.when(jnp.logical_not(at_home))
    def _():
        wait_for(x_in, dsend.at[3])

    @pl.when(core == 0)
    def _():
        span_ref = metric.at[pl.ds(0, 7)]
        pltpu.make_async_copy(span_ref, span_ref, msend.at[0]).wait()

    @pl.when(core == 1)
    def _():
        span_ref = metric.at[pl.ds(0, 8)]
        pltpu.make_async_copy(span_ref, span_ref, msend.at[0]).wait()

    pltpu.make_async_copy(three, three, msend.at[1]).wait()
    pltpu.make_async_copy(four, four, msend.at[2]).wait()
    pltpu.make_async_copy(eight, eight, msend.at[3]).wait()
    others = recv.at[pl.ds(0, 127)]
    pltpu.make_async_copy(others, others, ssem).wait()


def window_call(raw, root, vir, occ, kpoint, count):
    aux = root.shape[1]
    width = 2 * vir.shape[1]
    nvir = vir.shape[1]
    bf16, f32 = jnp.bfloat16, jnp.float32
    dma = pltpu.SemaphoreType.DMA
    vmem = pl.BlockSpec(memory_space=pltpu.VMEM)
    smem = pl.BlockSpec(memory_space=pltpu.SMEM)
    return pl.pallas_call(
        window_kernel,
        name="window",
        out_shape=(jax.ShapeDtypeStruct((aux, 2, width // 2), bf16), jax.ShapeDtypeStruct((9, 128), f32)),
        in_specs=[vmem, vmem, vmem, smem, smem, smem],
        out_specs=(vmem, vmem),
        scratch_shapes=[
            pltpu.VMEM((128,) + raw.shape[1:2] + raw.shape[3:], bf16),
            pltpu.VMEM((128,) + root.shape, bf16),
            pltpu.VMEM((aux, aux), bf16),
            pltpu.VMEM((aux, width), bf16),
            pltpu.VMEM((aux, width), bf16),
            pltpu.VMEM((width, aux), bf16),
            pltpu.VMEM((aux, width), bf16),
            pltpu.VMEM((aux, width), bf16),
            pltpu.VMEM((WINDOW, aux, width), bf16),
            pltpu.VMEM((WINDOW, width, width), f32),
            pltpu.VMEM((nvir, 128), f32),
            pltpu.VMEM((aux, width), f32),
            pltpu.VMEM((nvir, nvir), f32),
            pltpu.VMEM((2, nvir, width), bf16),
            pltpu.VMEM((2, nvir, width), bf16),
            pltpu.VMEM((4, nvir // 8, nvir), f32),
            pltpu.VMEM((4, nvir // 8, nvir), f32),
            pltpu.VMEM((3, nvir // 8, nvir), f32),
            pltpu.VMEM((nvir // 8, nvir), f32),
            pltpu.VMEM((16, 9, 128), f32),
            pltpu.VMEM((15, 9, 128), f32),
            pltpu.VMEM((9, 128), f32),
            pltpu.VMEM((4, 9, 128), f32),
            dma,
            dma((2, CHUNKS)),
            dma,
            dma((2, CHUNKS)),
            dma,
            dma((2, CHUNKS)),
            dma,
            dma,
            dma((2, CHUNKS)),
            dma,
            dma((4,)),
            dma((4,)),
            dma((4,)),
            dma,
            dma,
            dma((4,)),
            dma((4,)),
        ],
        compiler_params=pltpu.CompilerParams(
            collective_id=0, has_side_effects=True, vmem_limit_bytes=60000 * 1024
        ),
    )(raw, root, vir, occ, kpoint, count)


def shards(raw_ints, metric_root, occ_energy, vir_energy, block_kpoint, occ_count):
    nvir = raw_ints.shape[4]
    aux = metric_root.shape[1]
    gamma, piece = window_call(raw_ints, metric_root, vir_energy, occ_energy, block_kpoint, occ_count)
    share = 3 * nvir // 4
    density = lax.dynamic_slice(piece.reshape(-1), (lax.axis_index("narrow") * share,), (share,))
    return gamma.reshape(1, aux, 1, 2, nvir), density


def solution(mesh):
    placed = (P("narrow", "wide", None, None, None), P("wide", None), P(), P(), P(), P())
    return jax.shard_map(
        shards,
        mesh=mesh,
        in_specs=placed,
        out_specs=(P("narrow", None, "wide", None, None), P(("wide", "narrow"))),
        check_vma=False,
    )
```

```python
import functools

import jax
import jax.numpy as jnp
from jax import lax
from jax.experimental import pallas as pl
from jax.experimental.pallas import tpu as pltpu

from jax.sharding import PartitionSpec as P

MESH_ID = pl.DeviceIdType.MESH


def split_wide(w):
    return w // 64, (w // 16) % 4, w % 16


def join_wide(x, y, z):
    return x * 64 + y * 16 + z


def slot_of(w):
    x, y, z = split_wide(w)
    return x * 64 + y * 16 + (z % 2) * 8 + z // 2


def peer_at(step, w):
    x, y, z = split_wide(w)
    turn, side = step // 8, step % 8
    half = (turn + 1) // 2
    dz = jnp.where(turn % 2 == 1, half, 16 - half)
    return join_wide((x + side // 4) % 2, (y + side % 4) % 4, (z + dz) % 16)


CHUNKS = 4
WINDOW = 3


def add_up(ref, count):
    total = ref[0].astype(jnp.float32)
    for k in range(1, count):
        total = total + ref[k].astype(jnp.float32)
    return total


def window_kernel(
    raw, root, vir, occ, kpoint, count,
    gamma, piece,
    recv, metric, root_t, rows_in, own, own_t, relay, transit, far, table, column, total, dens, amp, mix,
    core_in, y_out, y_in, z_sum, z_all, z_out, z_in, x_out, x_in,
    own_sent, relay_in, relay_sent, near_in, near_sent, next_in, next_sent, last_in, turn_in, turn_sent, core_got, dsend, drecv, ssem, rsem, msend, mrecv,
):
    aux, width = own.shape
    nvir = vir.shape[1]
    half_rows = aux // 2
    rows = half_rows // (CHUNKS // 2)
    w = lax.axis_index("wide")
    n = lax.axis_index("narrow")
    core, x_hi = n % 2, n // 2
    x_lo, y, z = split_wide(w)
    x = 2 * x_hi + x_lo
    ahead, behind = (w + 127) % 128, (w + 1) % 128

    def along_x(step):
        there = (x + step) % 4
        return join_wide(there % 2, y, z), 2 * (there // 2) + core

    x_next, x_prev = along_x(1), along_x(3)
    sibling = (w, n + 1 - 2 * core)
    barrier = pltpu.get_barrier_semaphore()

    def greet(device):
        pl.semaphore_signal(barrier, inc=1, device_id=device, device_id_type=MESH_ID)

    def greet_wide(step, carry):
        greet(((w + step) % 128, n))
        return carry

    lax.fori_loop(1, 128, greet_wide, 0)
    for device in (x_next, x_prev, sibling):
        greet(device)
    at_home = core == x_lo
    targets = [(join_wide(core, y, z), k) for k in range(4)]
    sources = [(join_wide(k % 2, y, z), 2 * (k // 2) + x_lo) for k in range(4)]
    for device in targets + sources:

        @pl.when(jnp.logical_not(jnp.logical_and(device[0] == w, device[1] == n)))
        def _(device=device):
            greet(device)

    corner = jnp.logical_and(y == 0, z == 0)
    turned = join_wide(1 - x_lo, y, z)

    pl.semaphore_wait(barrier, 138 - 2 * at_home.astype(jnp.int32))

    slot = slot_of(w)
    par = (z + core) % 2

    def send_metric(step, carry):
        dz = 2 * step + core

        @pl.when(dz != 0)
        def _():
            pltpu.make_async_remote_copy(
                root, metric.at[slot], msend.at[0], mrecv.at[0],
                device_id=(join_wide(x_lo, y, (z + dz) % 16), n), device_id_type=MESH_ID,
            ).start()

        @pl.when(dz == 0)
        def _():
            pltpu.make_async_copy(root, metric.at[slot], mrecv.at[0]).start()

        return carry

    lax.fori_loop(0, 8, send_metric, 0)
    pltpu.make_async_copy(raw.at[0, :, w], recv.at[slot], rsem).start()

    def send_raw(step, carry):
        peer = peer_at(step, w)

        @pl.when(peer != w)
        def _():
            pltpu.make_async_remote_copy(
                raw.at[0, :, peer], recv.at[slot], ssem, rsem, device_id=(peer, n), device_id_type=MESH_ID
            ).start()

        return carry

    lax.fori_loop(0, 128, send_raw, 0)

    def part(side, k):
        start = side * half_rows + k % 2 * rows
        return pl.ds(pl.multiple_of(start, rows), rows), pl.ds(pl.multiple_of(k // 2 * nvir, 128), nvir)

    def send_own(k):
        for side, device in enumerate((x_next, x_prev)):
            at = part(side, k)
            pltpu.make_async_remote_copy(
                own.at[at[0], at[1]], relay.at[at[0], at[1]], own_sent, relay_in.at[side, k], device_id=device, device_id_type=MESH_ID
            ).start()

    def wait_for(ref, sem):
        pltpu.make_async_copy(ref, ref, sem).wait()

    def pass_on(k):
        for side, device in enumerate((x_next, x_prev)):
            at = part(side, k)
            wait_for(relay.at[at[0], at[1]], relay_in.at[side, k])
            pltpu.make_async_remote_copy(
                relay.at[at[0], at[1]], far.at[0, at[0], at[1]], relay_sent, near_in.at[side, k], device_id=device, device_id_type=MESH_ID
            ).start()

            @pl.when(jnp.logical_and(corner, x_lo == side))
            def _(side=side, at=at):
                pltpu.make_async_remote_copy(
                    relay.at[at[0], at[1]], far.at[1, at[0], at[1]], near_sent, next_in.at[side, k],
                    device_id=(join_wide(x_lo, 3, 15), n), device_id_type=MESH_ID,
                ).start()

    def send_near(k):
        for side in range(2):
            at = part(side, k)
            wait_for(far.at[0, at[0], at[1]], near_in.at[side, k])

            @pl.when(jnp.logical_or(jnp.logical_not(corner), x_lo == side))
            def _(side=side, at=at):
                pltpu.make_async_remote_copy(
                    far.at[0, at[0], at[1]], far.at[1, at[0], at[1]], near_sent, next_in.at[side, k],
                    device_id=(ahead, n), device_id_type=MESH_ID,
                ).start()

    def send_next(k):
        for side in range(2):
            at = part(side, k)
            wait_for(far.at[1, at[0], at[1]], next_in.at[side, k])

            @pl.when(corner)
            def _(side=side, at=at):
                pltpu.make_async_remote_copy(
                    far.at[1, at[0], at[1]], transit.at[at[0], at[1]], next_sent, turn_in.at[side, k],
                    device_id=(turned, n), device_id_type=MESH_ID,
                ).start()

            @pl.when(jnp.logical_not(corner))
            def _(at=at):
                pltpu.make_async_remote_copy(
                    far.at[1, at[0], at[1]], far.at[2, at[0], at[1]], next_sent, last_in.at[k // 2], device_id=(ahead, n), device_id_type=MESH_ID
                ).start()

    def send_turned(k):
        for side in range(2):
            at = part(side, k)
            wait_for(transit.at[at[0], at[1]], turn_in.at[side, k])
            pltpu.make_async_remote_copy(
                transit.at[at[0], at[1]], far.at[2, at[0], at[1]], turn_sent, last_in.at[k // 2],
                device_id=(join_wide(x_lo, 3, 15), n), device_id_type=MESH_ID,
            ).start()

    line = metric.at[pl.ds(pl.multiple_of(x_lo * 64 + y * 16 + par * 8, 8), 8)]
    pltpu.make_async_copy(line, line, mrecv.at[0]).wait()
    for step in range(1, 4):
        pltpu.make_async_remote_copy(
            line, line, msend.at[1], mrecv.at[1],
            device_id=(join_wide(x_lo, (y + step) % 4, z), n), device_id_type=MESH_ID,
        ).start()
    three = metric.at[pl.ds(0, 24)]
    pltpu.make_async_copy(three, three, mrecv.at[1]).wait()
    copies = []
    for row in range(4):
        span_ref = metric.at[pl.ds(pl.multiple_of(x_lo * 64 + row * 16 + par * 8, 8), 8)]
        copies.append(pltpu.make_async_remote_copy(
            span_ref, span_ref, msend.at[2], mrecv.at[2],
            device_id=(join_wide(1 - x_lo, y, z), n), device_id_type=MESH_ID,
        ))
    for copy in copies:
        copy.start()
    four = metric.at[pl.ds(0, 32)]
    pltpu.make_async_copy(four, four, mrecv.at[2]).wait()
    for row in range(8):
        span_ref = metric.at[pl.ds(pl.multiple_of(row * 16 + par * 8, 8), 8)]
        pltpu.make_async_remote_copy(
            span_ref, span_ref, msend.at[3], mrecv.at[3], device_id=sibling, device_id_type=MESH_ID
        ).start()
    eight = metric.at[pl.ds(0, 64)]
    pltpu.make_async_copy(eight, eight, mrecv.at[3]).wait()

    partner = (n + 2) % 4
    column[...] = jnp.broadcast_to(vir[pl.ds(n, 1), :], (128, nvir)).T
    partner_row = vir[pl.ds(partner, 1), :]
    total[...] = jnp.zeros_like(total)
    dens[...] = jnp.zeros_like(dens)
    for q in range(5):
        root_t[:, q * 128 : (q + 1) * 128] = metric[:, q, :].T

    def fill_table(s):
        there = (w + s) % 128
        for i in range(2):
            for j in range(2):
                level = occ[kpoint[n, w], i] + occ[kpoint[partner, there], j]
                alive = jnp.where(i < count[n, w], 1.0, 0.0) * jnp.where(j < count[partner, there], 1.0, 0.0)

                def some_rows(k, carry, i=i, j=j, level=level, alive=alive):
                    at = pl.multiple_of(k * 64, 64)
                    left = level - column[pl.ds(at, 64), :]
                    for c in range(nvir // 128):
                        gap = left - partner_row[:, c * 128 : (c + 1) * 128]
                        table[s, pl.ds(i * nvir + at, 64), j * nvir + c * 128 : j * nvir + (c + 1) * 128] = alive / gap
                    return carry

                lax.fori_loop(0, nvir // 64, some_rows, 0)

    def table_of(k, carry):
        fill_table(k)
        return carry

    lax.fori_loop(0, WINDOW, table_of, 0)
    pltpu.make_async_copy(recv, recv, rsem).wait()
    for q in range(5):
        for o in range(2):
            rows_in[q * 128 : (q + 1) * 128, o * nvir : (o + 1) * nvir] = recv[:, q, o, :]

    def fit(k, carry):
        at = pl.ds(pl.multiple_of(k * 128, 128), 128)
        own[at, :] = jnp.dot(root_t[at, :], rows_in[...], preferred_element_type=jnp.float32).astype(own.dtype)
        return carry

    lax.fori_loop(0, aux // 128, fit, 0)
    send_own(0)
    send_own(1)
    own_t[...] = own[...].T

    def round_of(k, carry):
        pass_on(k)

        @pl.when(k < CHUNKS - 2)
        def _():
            send_own(k + 2)

        @pl.when(k >= 1)
        def _():
            send_near(k - 1)

        return carry

    lax.fori_loop(0, CHUNKS, round_of, 0)
    send_near(CHUNKS - 1)

    def last_round(k, carry):
        send_next(k)

        @pl.when(corner)
        def _():
            send_turned(k)

        return carry

    lax.fori_loop(0, CHUNKS, last_round, 0)

    def add_gamma(s):
        for i in range(2):
            cols = slice(i * nvir, (i + 1) * nvir)
            total[:, cols] += lax.dot_general(
                far[s], mix[i], (((1,), (1,)), ((), ())), preferred_element_type=jnp.float32
            )

    def window_step(s, carry):
        for j in range(2):
            cols = slice(j * nvir, (j + 1) * nvir)

            @pl.when(s == WINDOW - 1)
            def _(j=j, cols=cols):
                wait_for(far.at[2, :, cols], last_in.at[j])

            for i in range(2):
                left = own_t[i * nvir : (i + 1) * nvir, :]
                product = jnp.dot(left, far[s, :, cols], preferred_element_type=jnp.float32)
                amplitude = product * table[s, i * nvir : (i + 1) * nvir, cols]
                half = amplitude.astype(jnp.bfloat16)
                amp[i, :, cols] = half
                mixed = 2.0 * amplitude - half.T.astype(jnp.float32)
                mix[i, :, cols] = mixed.astype(jnp.bfloat16)
        for i in range(2):
            dens[...] += lax.dot_general(
                mix[i], amp[i], (((1,), (1,)), ((), ())), preferred_element_type=jnp.float32
            )

        @pl.when(s < WINDOW - 1)
        def _():
            add_gamma(s)

        return carry

    lax.fori_loop(0, WINDOW, window_step, 0)

    span = nvir // 8

    def share(of_core, row):
        return dens.at[pl.ds(pl.multiple_of(of_core * 4 * span + row * span, span), span)]

    order = [(y + step) % 4 for step in (2, 1, 3, 0)]
    for row in order:
        pltpu.make_async_remote_copy(
            share(1 - core, row), core_in.at[row], dsend.at[0], core_got.at[row],
            device_id=sibling, device_id_type=MESH_ID,
        ).start()
    for step, row in zip((2, 1, 3), order):
        wait_for(core_in.at[row], core_got.at[row])
        y_out[row] = (share(core, row)[...] + core_in[row]).astype(y_out.dtype)
        pltpu.make_async_remote_copy(
            y_out.at[row], y_in.at[step - 1], dsend.at[1], drecv.at[1],
            device_id=(join_wide(x_lo, row, z), n), device_id_type=MESH_ID,
        ).start()
    add_gamma(WINDOW - 1)
    wait_for(core_in.at[y], core_got.at[y])
    mine = share(core, y)[...] + core_in[y]
    wait_for(y_in, drecv.at[1])
    z_sum[...] = mine + add_up(y_in, 3)
    for k in range(16):
        for r in range(3):
            for c in range(3):
                z_all[k, 3 * r + c : 3 * r + c + 1, :] = z_sum[3 * k + r : 3 * k + r + 1, c * 128 : (c + 1) * 128]
    z_out[...] = z_all[...].astype(z_out.dtype)
    for step in range(1, 16):
        to = (z + step) % 16
        pltpu.make_async_remote_copy(
            z_out.at[to], z_in.at[step - 1], dsend.at[2], drecv.at[2],
            device_id=(join_wide(x_lo, y, to), n), device_id_type=MESH_ID,
        ).start()
    for i in range(2):
        gamma[:, i, :] = total[:, i * nvir : (i + 1) * nvir].astype(gamma.dtype)
    wait_for(z_in, drecv.at[2])
    x_out[...] = z_all[z] + add_up(z_in, 15)
    for device in targets:
        here = jnp.logical_and(device[0] == w, device[1] == n)

        @pl.when(here)
        def _():
            pltpu.make_async_copy(x_out, x_in.at[x], drecv.at[3]).start()

        @pl.when(jnp.logical_not(here))
        def _(device=device):
            pltpu.make_async_remote_copy(
                x_out, x_in.at[x], dsend.at[3], drecv.at[3], device_id=device, device_id_type=MESH_ID
            ).start()

    wait_for(x_in, drecv.at[3])
    piece[...] = add_up(x_in, 4) * (1.0 / (4 * 128 * nvir))

    wait_for(own, own_sent)
    wait_for(own, relay_sent)
    wait_for(own, near_sent)
    wait_for(own, next_sent)

    @pl.when(corner)
    def _():
        wait_for(transit, turn_sent)

    wait_for(core_in, dsend.at[0])
    wait_for(y_in, dsend.at[1])
    wait_for(z_in, dsend.at[2])

    @pl.when(at_home)
    def _():
        wait_for(x_in.at[pl.ds(0, 3)], dsend.at[3])

    @pl.when(jnp.logical_not(at_home))
    def _():
        wait_for(x_in, dsend.at[3])

    @pl.when(core == 0)
    def _():
        span_ref = metric.at[pl.ds(0, 7)]
        pltpu.make_async_copy(span_ref, span_ref, msend.at[0]).wait()

    @pl.when(core == 1)
    def _():
        span_ref = metric.at[pl.ds(0, 8)]
        pltpu.make_async_copy(span_ref, span_ref, msend.at[0]).wait()

    pltpu.make_async_copy(three, three, msend.at[1]).wait()
    pltpu.make_async_copy(four, four, msend.at[2]).wait()
    pltpu.make_async_copy(eight, eight, msend.at[3]).wait()
    others = recv.at[pl.ds(0, 127)]
    pltpu.make_async_copy(others, others, ssem).wait()


def window_call(raw, root, vir, occ, kpoint, count):
    aux = root.shape[1]
    width = 2 * vir.shape[1]
    nvir = vir.shape[1]
    bf16, f32 = jnp.bfloat16, jnp.float32
    dma = pltpu.SemaphoreType.DMA
    vmem = pl.BlockSpec(memory_space=pltpu.VMEM)
    smem = pl.BlockSpec(memory_space=pltpu.SMEM)
    return pl.pallas_call(
        window_kernel,
        name="window",
        out_shape=(jax.ShapeDtypeStruct((aux, 2, width // 2), bf16), jax.ShapeDtypeStruct((9, 128), f32)),
        in_specs=[vmem, vmem, vmem, smem, smem, smem],
        out_specs=(vmem, vmem),
        scratch_shapes=[
            pltpu.VMEM((128,) + raw.shape[1:2] + raw.shape[3:], bf16),
            pltpu.VMEM((128,) + root.shape, bf16),
            pltpu.VMEM((aux, aux), bf16),
            pltpu.VMEM((aux, width), bf16),
            pltpu.VMEM((aux, width), bf16),
            pltpu.VMEM((width, aux), bf16),
            pltpu.VMEM((aux, width), bf16),
            pltpu.VMEM((aux, width), bf16),
            pltpu.VMEM((WINDOW, aux, width), bf16),
            pltpu.VMEM((WINDOW, width, width), f32),
            pltpu.VMEM((nvir, 128), f32),
            pltpu.VMEM((aux, width), f32),
            pltpu.VMEM((nvir, nvir), f32),
            pltpu.VMEM((2, nvir, width), bf16),
            pltpu.VMEM((2, nvir, width), bf16),
            pltpu.VMEM((4, nvir // 8, nvir), f32),
            pltpu.VMEM((4, nvir // 8, nvir), bf16),
            pltpu.VMEM((3, nvir // 8, nvir), bf16),
            pltpu.VMEM((nvir // 8, nvir), f32),
            pltpu.VMEM((16, 9, 128), f32),
            pltpu.VMEM((16, 9, 128), bf16),
            pltpu.VMEM((15, 9, 128), bf16),
            pltpu.VMEM((9, 128), f32),
            pltpu.VMEM((4, 9, 128), f32),
            dma,
            dma((2, CHUNKS)),
            dma,
            dma((2, CHUNKS)),
            dma,
            dma((2, CHUNKS)),
            dma,
            dma((2,)),
            dma((2, CHUNKS)),
            dma,
            dma((4,)),
            dma((4,)),
            dma((4,)),
            dma,
            dma,
            dma((4,)),
            dma((4,)),
        ],
        compiler_params=pltpu.CompilerParams(
            collective_id=0, has_side_effects=True, vmem_limit_bytes=60000 * 1024
        ),
    )(raw, root, vir, occ, kpoint, count)


def finish_kernel(gamma, piece, gamma_out, density, sem):
    copy = pltpu.make_async_copy(gamma, gamma_out, sem)
    copy.start()
    n = lax.axis_index("narrow")
    for k in range(4):

        @pl.when(n == k)
        def _(k=k):
            cut = 32 * k
            for r in range(3):
                row = piece[2 * k + r : 2 * k + r + 1, cut:]
                if cut and 2 * k + r + 1 < 9:
                    row = jnp.concatenate([row, piece[2 * k + r + 1 : 2 * k + r + 2, :cut]], axis=1)
                size = 128 if r < 2 else 32
                density[r * 128 : r * 128 + size] = row[0, :size]

    copy.wait()


def finish(gamma, piece):
    vmem = pl.BlockSpec(memory_space=pltpu.VMEM)
    return pl.pallas_call(
        finish_kernel,
        name="finish",
        out_shape=(jax.ShapeDtypeStruct(gamma.shape, gamma.dtype), jax.ShapeDtypeStruct((288,), jnp.float32)),
        in_specs=[vmem, vmem],
        out_specs=(pl.BlockSpec(memory_space=pl.ANY), vmem),
        scratch_shapes=[pltpu.SemaphoreType.DMA],
    )(gamma, piece)


def shards(raw_ints, metric_root, occ_energy, vir_energy, block_kpoint, occ_count):
    nvir = raw_ints.shape[4]
    aux = metric_root.shape[1]
    gamma, piece = window_call(raw_ints, metric_root, vir_energy, occ_energy, block_kpoint, occ_count)
    gamma, density = finish(gamma, piece)
    return gamma.reshape(1, aux, 1, 2, nvir), density


def solution(mesh):
    placed = (P("narrow", "wide", None, None, None), P("wide", None), P(), P(), P(), P())
    return jax.shard_map(
        shards,
        mesh=mesh,
        in_specs=placed,
        out_specs=(P("narrow", None, "wide", None, None), P(("wide", "narrow"))),
        check_vma=False,
    )
```

```python
import functools

import jax
import jax.numpy as jnp
from jax import lax
from jax.experimental import pallas as pl
from jax.experimental.pallas import tpu as pltpu

from jax.sharding import PartitionSpec as P

MESH_ID = pl.DeviceIdType.MESH


def split_wide(w):
    return w // 64, (w // 16) % 4, w % 16


def join_wide(x, y, z):
    return x * 64 + y * 16 + z


def slot_of(w):
    x, y, z = split_wide(w)
    return x * 64 + y * 16 + (z % 2) * 8 + z // 2


def peer_at(step, w):
    x, y, z = split_wide(w)
    turn, side = step // 8, step % 8
    half = (turn + 1) // 2
    dz = jnp.where(turn % 2 == 1, half, 16 - half)
    return join_wide((x + side // 4) % 2, (y + side % 4) % 4, (z + dz) % 16)


SHARES = 4
CHUNKS = 2 * SHARES
GROUP = 32
WINDOW = 3


def add_up(ref, count):
    total = ref[0].astype(jnp.float32)
    for k in range(1, count):
        total = total + ref[k].astype(jnp.float32)
    return total


def window_kernel(
    raw, root, vir, occ, kpoint, count,
    gamma, piece,
    recv, metric, arranged, root_rows, root_t, rows_in, own, own_t, relay, transit, far, table, column, total, dens, amp, mix,
    core_in, y_out, y_in, z_sum, z_all, z_out, z_in, x_out, x_in,
    own_sent, relay_in, relay_sent, near_in, near_sent, next_in, next_sent, last_in, turn_in, turn_sent, core_got, dsend, drecv, ssem, rsem, msend, mrecv,
):
    _, aux, _ = own.shape
    nvir = vir.shape[1]
    half_rows = aux // 2
    rows = half_rows // SHARES
    w = lax.axis_index("wide")
    n = lax.axis_index("narrow")
    core, x_hi = n % 2, n // 2
    x_lo, y, z = split_wide(w)
    x = 2 * x_hi + x_lo
    ahead, behind = (w + 127) % 128, (w + 1) % 128

    def along_x(step):
        there = (x + step) % 4
        return join_wide(there % 2, y, z), 2 * (there // 2) + core

    x_next, x_prev = along_x(1), along_x(3)
    sibling = (w, n + 1 - 2 * core)
    barrier = pltpu.get_barrier_semaphore()

    def greet(device):
        pl.semaphore_signal(barrier, inc=1, device_id=device, device_id_type=MESH_ID)

    def greet_wide(step, carry):
        greet(((w + step) % 128, n))
        return carry

    lax.fori_loop(1, 128, greet_wide, 0)
    for device in (x_next, x_prev, sibling):
        greet(device)
    at_home = core == x_lo
    targets = [(join_wide(core, y, z), k) for k in range(4)]
    sources = [(join_wide(k % 2, y, z), 2 * (k // 2) + x_lo) for k in range(4)]
    for device in targets + sources:

        @pl.when(jnp.logical_not(jnp.logical_and(device[0] == w, device[1] == n)))
        def _(device=device):
            greet(device)

    corner = jnp.logical_and(y == 0, z == 0)
    turned = join_wide(1 - x_lo, y, z)

    pl.semaphore_wait(barrier, 138 - 2 * at_home.astype(jnp.int32))

    slot = slot_of(w)
    par = (z + core) % 2

    def send_metric(step, carry):
        dz = 2 * step + core

        @pl.when(dz != 0)
        def _():
            pltpu.make_async_remote_copy(
                root, metric.at[slot], msend.at[0], mrecv.at[0],
                device_id=(join_wide(x_lo, y, (z + dz) % 16), n), device_id_type=MESH_ID,
            ).start()

        @pl.when(dz == 0)
        def _():
            pltpu.make_async_copy(root, metric.at[slot], mrecv.at[0]).start()

        return carry

    lax.fori_loop(0, 8, send_metric, 0)
    pltpu.make_async_copy(raw.at[0, :, w], recv.at[0], rsem.at[0]).start()

    def send_raw(step, carry):
        peer = peer_at(step, w)

        @pl.when(peer != w)
        def _():
            pltpu.make_async_remote_copy(
                raw.at[0, :, peer], recv.at[step], ssem, rsem.at[step // GROUP], device_id=(peer, n),
                device_id_type=MESH_ID,
            ).start()

        return carry

    lax.fori_loop(0, 128, send_raw, 0)

    def part(side, k):
        start = side * half_rows + k % SHARES * rows
        return k // SHARES, pl.ds(pl.multiple_of(start, rows), rows)

    def send_own(k):
        for side, device in enumerate((x_next, x_prev)):
            at = part(side, k)
            pltpu.make_async_remote_copy(
                own.at[at[0], at[1]], relay.at[at[0], at[1]], own_sent, relay_in.at[side, k], device_id=device, device_id_type=MESH_ID
            ).start()

    def wait_for(ref, sem):
        pltpu.make_async_copy(ref, ref, sem).wait()

    def pass_on(k):
        for side, device in enumerate((x_next, x_prev)):
            at = part(side, k)
            wait_for(relay.at[at[0], at[1]], relay_in.at[side, k])
            pltpu.make_async_remote_copy(
                relay.at[at[0], at[1]], far.at[0, at[0], at[1]], relay_sent, near_in.at[side, k], device_id=device, device_id_type=MESH_ID
            ).start()

            @pl.when(jnp.logical_and(corner, x_lo == side))
            def _(side=side, at=at):
                pltpu.make_async_remote_copy(
                    relay.at[at[0], at[1]], far.at[1, at[0], at[1]], near_sent, next_in.at[side, k],
                    device_id=(join_wide(x_lo, 3, 15), n), device_id_type=MESH_ID,
                ).start()

    def send_near(k):
        for side in range(2):
            at = part(side, k)
            wait_for(far.at[0, at[0], at[1]], near_in.at[side, k])

            @pl.when(jnp.logical_or(jnp.logical_not(corner), x_lo == side))
            def _(side=side, at=at):
                pltpu.make_async_remote_copy(
                    far.at[0, at[0], at[1]], far.at[1, at[0], at[1]], near_sent, next_in.at[side, k],
                    device_id=(ahead, n), device_id_type=MESH_ID,
                ).start()

    def send_next(k):
        for side in range(2):
            at = part(side, k)
            wait_for(far.at[1, at[0], at[1]], next_in.at[side, k])

            @pl.when(corner)
            def _(side=side, at=at):
                pltpu.make_async_remote_copy(
                    far.at[1, at[0], at[1]], transit.at[at[0], at[1]], next_sent, turn_in.at[side, k],
                    device_id=(turned, n), device_id_type=MESH_ID,
                ).start()

            @pl.when(jnp.logical_not(corner))
            def _(at=at):
                pltpu.make_async_remote_copy(
                    far.at[1, at[0], at[1]], far.at[2, at[0], at[1]], next_sent, last_in.at[k // SHARES], device_id=(ahead, n), device_id_type=MESH_ID
                ).start()

    def send_turned(k):
        for side in range(2):
            at = part(side, k)
            wait_for(transit.at[at[0], at[1]], turn_in.at[side, k])
            pltpu.make_async_remote_copy(
                transit.at[at[0], at[1]], far.at[2, at[0], at[1]], turn_sent, last_in.at[k // SHARES],
                device_id=(join_wide(x_lo, 3, 15), n), device_id_type=MESH_ID,
            ).start()

    line = metric.at[pl.ds(pl.multiple_of(x_lo * 64 + y * 16 + par * 8, 8), 8)]
    pltpu.make_async_copy(line, line, mrecv.at[0]).wait()
    for step in range(1, 4):
        pltpu.make_async_remote_copy(
            line, line, msend.at[1], mrecv.at[1],
            device_id=(join_wide(x_lo, (y + step) % 4, z), n), device_id_type=MESH_ID,
        ).start()
    three = metric.at[pl.ds(0, 24)]
    pltpu.make_async_copy(three, three, mrecv.at[1]).wait()
    copies = []
    for row in range(4):
        span_ref = metric.at[pl.ds(pl.multiple_of(x_lo * 64 + row * 16 + par * 8, 8), 8)]
        copies.append(pltpu.make_async_remote_copy(
            span_ref, span_ref, msend.at[2], mrecv.at[2],
            device_id=(join_wide(1 - x_lo, y, z), n), device_id_type=MESH_ID,
        ))
    for copy in copies:
        copy.start()
    four = metric.at[pl.ds(0, 32)]
    pltpu.make_async_copy(four, four, mrecv.at[2]).wait()
    for row in range(8):
        span_ref = metric.at[pl.ds(pl.multiple_of(row * 16 + par * 8, 8), 8)]
        pltpu.make_async_remote_copy(
            span_ref, span_ref, msend.at[3], mrecv.at[3], device_id=sibling, device_id_type=MESH_ID
        ).start()
    eight = metric.at[pl.ds(0, 64)]
    pltpu.make_async_copy(eight, eight, mrecv.at[3]).wait()

    partner = (n + 2) % 4
    column[...] = jnp.broadcast_to(vir[pl.ds(n, 1), :], (128, nvir)).T
    partner_row = vir[pl.ds(partner, 1), :]
    dens[...] = jnp.zeros_like(dens)

    def reorder(step, carry):
        turn, side = step // 8, step % 8
        half = (turn + 1) // 2
        dz = jnp.where(turn % 2 == 1, 16 - half, half)
        source = join_wide((x_lo + side // 4) % 2, (y + 4 - side % 4) % 4, (z + dz) % 16)
        arranged[step] = metric[slot_of(source)]
        return carry

    lax.fori_loop(0, 128, reorder, 0)
    for g in range(128 // GROUP):
        for q in range(5):
            root_rows[q * GROUP : (q + 1) * GROUP, :] = arranged[g * GROUP : (g + 1) * GROUP, q, :]
        root_t[g] = root_rows[...].T

    def fill_table(s):
        there = (w + s) % 128
        for i in range(2):
            for j in range(2):
                level = occ[i, kpoint[n, w]] + occ[j, kpoint[partner, there]]
                alive = jnp.where(i < count[n, w], 1.0, 0.0) * jnp.where(j < count[partner, there], 1.0, 0.0)

                def some_rows(k, carry, i=i, j=j, level=level, alive=alive):
                    at = pl.multiple_of(k * 64, 64)
                    left = level - column[pl.ds(at, 64), :]
                    for c in range(nvir // 128):
                        gap = left - partner_row[:, c * 128 : (c + 1) * 128]
                        table[s, pl.ds(i * nvir + at, 64), j * nvir + c * 128 : j * nvir + (c + 1) * 128] = alive / gap
                    return carry

                lax.fori_loop(0, nvir // 64, some_rows, 0)

    def table_of(k, carry):
        fill_table(k)
        return carry

    lax.fori_loop(0, WINDOW, table_of, 0)
    for g in range(128 // GROUP):
        arrived = recv.at[pl.ds(g * GROUP, GROUP)]
        wait_for(arrived, rsem.at[g])
        for o in range(2):
            cols = slice(o * nvir, (o + 1) * nvir)
            for q in range(5):
                rows_in[q * GROUP : (q + 1) * GROUP, cols] = recv[g * GROUP : (g + 1) * GROUP, q, o, :]
            for k in range(5):
                at = slice(k * aux // 5, (k + 1) * aux // 5)
                term = jnp.dot(root_t[g, at, :], rows_in[:, cols], preferred_element_type=jnp.float32)
                if g == 0:
                    total[at, cols] = term
                elif g < 128 // GROUP - 1:
                    total[at, cols] += term
                else:
                    own[o, at, :] = (total[at, cols] + term).astype(own.dtype)
            if g == 128 // GROUP - 1 and o == 0:
                send_own(0)
                send_own(1)
    for o in range(2):
        own_t[o * nvir : (o + 1) * nvir, :] = own[o].T
    total[...] = jnp.zeros_like(total)

    def round_of(k, carry):
        pass_on(k)

        @pl.when(k < CHUNKS - 2)
        def _():
            send_own(k + 2)

        @pl.when(k >= 1)
        def _():
            send_near(k - 1)

        return carry

    lax.fori_loop(0, CHUNKS, round_of, 0)
    send_near(CHUNKS - 1)

    def last_round(k, carry):
        send_next(k)

        @pl.when(corner)
        def _():
            send_turned(k)

        return carry

    lax.fori_loop(0, CHUNKS, last_round, 0)

    def add_gamma(s):
        for i in range(2):
            cols = slice(i * nvir, (i + 1) * nvir)
            for j in range(2):
                total[:, cols] += lax.dot_general(
                    far[s, j], mix[i, :, j * nvir : (j + 1) * nvir], (((1,), (1,)), ((), ())),
                    preferred_element_type=jnp.float32,
                )

    def window_step(s, carry):
        for j in range(2):
            cols = slice(j * nvir, (j + 1) * nvir)

            @pl.when(s == WINDOW - 1)
            def _(j=j, cols=cols):
                wait_for(far.at[2, j], last_in.at[j])

            for i in range(2):
                left = own_t[i * nvir : (i + 1) * nvir, :]
                product = jnp.dot(left, far[s, j], preferred_element_type=jnp.float32)
                amplitude = product * table[s, i * nvir : (i + 1) * nvir, cols]
                half = amplitude.astype(jnp.bfloat16)
                amp[i, :, cols] = half
                mixed = 2.0 * amplitude - half.T.astype(jnp.float32)
                mix[i, :, cols] = mixed.astype(jnp.bfloat16)
        for i in range(2):
            dens[...] += lax.dot_general(
                mix[i], amp[i], (((1,), (1,)), ((), ())), preferred_element_type=jnp.float32
            )

        @pl.when(s < WINDOW - 1)
        def _():
            add_gamma(s)

        return carry

    lax.fori_loop(0, WINDOW, window_step, 0)

    span = nvir // 8

    def share(of_core, row):
        return dens.at[pl.ds(pl.multiple_of(of_core * 4 * span + row * span, span), span)]

    order = [(y + step) % 4 for step in (2, 1, 3, 0)]
    for row in order:
        pltpu.make_async_remote_copy(
            share(1 - core, row), core_in.at[row], dsend.at[0], core_got.at[row],
            device_id=sibling, device_id_type=MESH_ID,
        ).start()
    for step, row in zip((2, 1, 3), order):
        wait_for(core_in.at[row], core_got.at[row])
        y_out[row] = (share(core, row)[...] + core_in[row]).astype(y_out.dtype)
        pltpu.make_async_remote_copy(
            y_out.at[row], y_in.at[step - 1], dsend.at[1], drecv.at[1],
            device_id=(join_wide(x_lo, row, z), n), device_id_type=MESH_ID,
        ).start()
    add_gamma(WINDOW - 1)
    wait_for(core_in.at[y], core_got.at[y])
    mine = share(core, y)[...] + core_in[y]
    wait_for(y_in, drecv.at[1])
    z_sum[...] = mine + add_up(y_in, 3)
    for k in range(16):
        for r in range(3):
            for c in range(3):
                z_all[k, 3 * r + c : 3 * r + c + 1, :] = z_sum[3 * k + r : 3 * k + r + 1, c * 128 : (c + 1) * 128]
    z_out[...] = z_all[...].astype(z_out.dtype)
    for step in range(1, 16):
        to = (z + step) % 16
        pltpu.make_async_remote_copy(
            z_out.at[to], z_in.at[step - 1], dsend.at[2], drecv.at[2],
            device_id=(join_wide(x_lo, y, to), n), device_id_type=MESH_ID,
        ).start()
    for i in range(2):
        gamma[:, i, :] = total[:, i * nvir : (i + 1) * nvir].astype(gamma.dtype)
    wait_for(z_in, drecv.at[2])
    x_out[...] = z_all[z] + add_up(z_in, 15)
    for device in targets:
        here = jnp.logical_and(device[0] == w, device[1] == n)

        @pl.when(here)
        def _():
            pltpu.make_async_copy(x_out, x_in.at[x], drecv.at[3]).start()

        @pl.when(jnp.logical_not(here))
        def _(device=device):
            pltpu.make_async_remote_copy(
                x_out, x_in.at[x], dsend.at[3], drecv.at[3], device_id=device, device_id_type=MESH_ID
            ).start()

    wait_for(x_in, drecv.at[3])
    piece[...] = add_up(x_in, 4) * (1.0 / (4 * 128 * nvir))

    wait_for(own, own_sent)
    wait_for(own, relay_sent)
    wait_for(own, near_sent)
    wait_for(own, next_sent)

    @pl.when(corner)
    def _():
        wait_for(transit, turn_sent)

    wait_for(core_in, dsend.at[0])
    wait_for(y_in, dsend.at[1])
    wait_for(z_in, dsend.at[2])

    @pl.when(at_home)
    def _():
        wait_for(x_in.at[pl.ds(0, 3)], dsend.at[3])

    @pl.when(jnp.logical_not(at_home))
    def _():
        wait_for(x_in, dsend.at[3])

    @pl.when(core == 0)
    def _():
        span_ref = metric.at[pl.ds(0, 7)]
        pltpu.make_async_copy(span_ref, span_ref, msend.at[0]).wait()

    @pl.when(core == 1)
    def _():
        span_ref = metric.at[pl.ds(0, 8)]
        pltpu.make_async_copy(span_ref, span_ref, msend.at[0]).wait()

    pltpu.make_async_copy(three, three, msend.at[1]).wait()
    pltpu.make_async_copy(four, four, msend.at[2]).wait()
    pltpu.make_async_copy(eight, eight, msend.at[3]).wait()
    others = recv.at[pl.ds(0, 127)]
    pltpu.make_async_copy(others, others, ssem).wait()


def window_call(raw, root, vir, occ, kpoint, count):
    aux = root.shape[1]
    width = 2 * vir.shape[1]
    nvir = vir.shape[1]
    bf16, f32 = jnp.bfloat16, jnp.float32
    dma = pltpu.SemaphoreType.DMA
    vmem = pl.BlockSpec(memory_space=pltpu.VMEM)
    smem = pl.BlockSpec(memory_space=pltpu.SMEM)
    return pl.pallas_call(
        window_kernel,
        name="window",
        out_shape=(jax.ShapeDtypeStruct((aux, 2, width // 2), bf16), jax.ShapeDtypeStruct((9, 128), f32)),
        in_specs=[vmem, vmem, vmem, smem, smem, smem],
        out_specs=(vmem, vmem),
        scratch_shapes=[
            pltpu.VMEM((128,) + raw.shape[1:2] + raw.shape[3:], bf16),
            pltpu.VMEM((128,) + root.shape, bf16),
            pltpu.VMEM((128,) + root.shape, bf16),
            pltpu.VMEM((5 * GROUP, aux), bf16),
            pltpu.VMEM((128 // GROUP, aux, 5 * GROUP), bf16),
            pltpu.VMEM((5 * GROUP, width), bf16),
            pltpu.VMEM((2, aux, nvir), bf16),
            pltpu.VMEM((width, aux), bf16),
            pltpu.VMEM((2, aux, nvir), bf16),
            pltpu.VMEM((2, aux, nvir), bf16),
            pltpu.VMEM((WINDOW, 2, aux, nvir), bf16),
            pltpu.VMEM((WINDOW, width, width), f32),
            pltpu.VMEM((nvir, 128), f32),
            pltpu.VMEM((aux, width), f32),
            pltpu.VMEM((nvir, nvir), f32),
            pltpu.VMEM((2, nvir, width), bf16),
            pltpu.VMEM((2, nvir, width), bf16),
            pltpu.VMEM((4, nvir // 8, nvir), f32),
            pltpu.VMEM((4, nvir // 8, nvir), bf16),
            pltpu.VMEM((3, nvir // 8, nvir), bf16),
            pltpu.VMEM((nvir // 8, nvir), f32),
            pltpu.VMEM((16, 9, 128), f32),
            pltpu.VMEM((16, 9, 128), bf16),
            pltpu.VMEM((15, 9, 128), bf16),
            pltpu.VMEM((9, 128), f32),
            pltpu.VMEM((4, 9, 128), f32),
            dma,
            dma((2, CHUNKS)),
            dma,
            dma((2, CHUNKS)),
            dma,
            dma((2, CHUNKS)),
            dma,
            dma((2,)),
            dma((2, CHUNKS)),
            dma,
            dma((4,)),
            dma((4,)),
            dma((4,)),
            dma,
            dma((128 // GROUP,)),
            dma((4,)),
            dma((4,)),
        ],
        compiler_params=pltpu.CompilerParams(
            collective_id=0, has_side_effects=True, vmem_limit_bytes=60000 * 1024
        ),
    )(raw, root, vir, occ, kpoint, count)


def finish_kernel(gamma, piece, gamma_out, density, sem):
    copy = pltpu.make_async_copy(gamma, gamma_out, sem)
    copy.start()
    n = lax.axis_index("narrow")
    for k in range(4):

        @pl.when(n == k)
        def _(k=k):
            cut = 32 * k
            for r in range(3):
                row = piece[2 * k + r : 2 * k + r + 1, cut:]
                if cut and 2 * k + r + 1 < 9:
                    row = jnp.concatenate([row, piece[2 * k + r + 1 : 2 * k + r + 2, :cut]], axis=1)
                size = 128 if r < 2 else 32
                density[r * 128 : r * 128 + size] = row[0, :size]

    copy.wait()


def finish(gamma, piece):
    vmem = pl.BlockSpec(memory_space=pltpu.VMEM)
    return pl.pallas_call(
        finish_kernel,
        name="finish",
        out_shape=(jax.ShapeDtypeStruct(gamma.shape, gamma.dtype), jax.ShapeDtypeStruct((288,), jnp.float32)),
        in_specs=[vmem, vmem],
        out_specs=(pl.BlockSpec(memory_space=pl.ANY), vmem),
        scratch_shapes=[pltpu.SemaphoreType.DMA],
    )(gamma, piece)


def shards(raw_ints, metric_root, occ_energy, vir_energy, block_kpoint, occ_count):
    nvir = raw_ints.shape[4]
    aux = metric_root.shape[1]
    gamma, piece = window_call(raw_ints, metric_root, vir_energy, occ_energy.T, block_kpoint, occ_count)
    gamma, density = finish(gamma, piece)
    return gamma.reshape(1, aux, 1, 2, nvir), density


def solution(mesh):
    placed = (P("narrow", "wide", None, None, None), P("wide", None), P(), P(), P(), P())
    return jax.shard_map(
        shards,
        mesh=mesh,
        in_specs=placed,
        out_specs=(P("narrow", None, "wide", None, None), P(("wide", "narrow"))),
        check_vma=False,
    )
```

```python
import functools

import jax
import jax.numpy as jnp
from jax import lax
from jax.experimental import pallas as pl
from jax.experimental.pallas import tpu as pltpu

from jax.sharding import PartitionSpec as P

MESH_ID = pl.DeviceIdType.MESH


def split_wide(w):
    return w // 64, (w // 16) % 4, w % 16


def join_wide(x, y, z):
    return x * 64 + y * 16 + z


def slot_of(w):
    x, y, z = split_wide(w)
    return x * 64 + y * 16 + (z % 2) * 8 + z // 2


def peer_at(step, w):
    x, y, z = split_wide(w)
    turn, side = 15 - step // 8, step % 8
    half = (turn + 1) // 2
    dz = jnp.where(turn % 2 == 1, half, 16 - half)
    return join_wide((x + side // 4) % 2, (y + side % 4) % 4, (z + dz) % 16)


SHARES = 4
CHUNKS = 2 * SHARES
AHEAD = 3
NEAR_LAG = 2
NEXT_LAG = 5
GROUP = 32
WINDOW = 3


def add_up(ref, count):
    total = ref[0].astype(jnp.float32)
    for k in range(1, count):
        total = total + ref[k].astype(jnp.float32)
    return total


def window_kernel(
    raw, root, vir, occ, kpoint, count,
    gamma, piece,
    leaving, recv, metric, arranged, root_rows, root_t, rows_in, own, own_t, relay, transit, far, table, column, total, dens, amp, mix,
    core_in, y_out, y_in, z_sum, z_all, z_out, z_in, x_out, x_in,
    own_sent, relay_in, relay_sent, near_in, near_sent, next_in, next_sent, last_in, turn_in, turn_sent, core_got, dsend, drecv, ssem, rsem, msend, mrecv, left_sem,
):
    _, aux, _ = own.shape
    nvir = vir.shape[1]
    half_rows = aux // 2
    rows = half_rows // SHARES
    w = lax.axis_index("wide")
    n = lax.axis_index("narrow")
    core, x_hi = n % 2, n // 2
    x_lo, y, z = split_wide(w)
    x = 2 * x_hi + x_lo
    ahead, behind = (w + 127) % 128, (w + 1) % 128

    def along_x(step):
        there = (x + step) % 4
        return join_wide(there % 2, y, z), 2 * (there // 2) + core

    x_next, x_prev = along_x(1), along_x(3)
    sibling = (w, n + 1 - 2 * core)
    barrier = pltpu.get_barrier_semaphore()

    def greet(device):
        pl.semaphore_signal(barrier, inc=1, device_id=device, device_id_type=MESH_ID)

    def greet_wide(step, carry):
        greet(((w + step) % 128, n))
        return carry

    lax.fori_loop(1, 128, greet_wide, 0)
    for device in (x_next, x_prev, sibling):
        greet(device)
    at_home = core == x_lo
    targets = [(join_wide(core, y, z), k) for k in range(4)]
    sources = [(join_wide(k % 2, y, z), 2 * (k // 2) + x_lo) for k in range(4)]
    for device in targets + sources:

        @pl.when(jnp.logical_not(jnp.logical_and(device[0] == w, device[1] == n)))
        def _(device=device):
            greet(device)

    corner = jnp.logical_and(y == 0, z == 0)
    turned = join_wide(1 - x_lo, y, z)

    pl.semaphore_wait(barrier, 138 - 2 * at_home.astype(jnp.int32))

    slot = slot_of(w)
    par = (z + core) % 2

    def send_metric(step, carry):
        dz = 2 * step + core

        @pl.when(dz != 0)
        def _():
            pltpu.make_async_remote_copy(
                root, metric.at[slot], msend.at[0], mrecv.at[0],
                device_id=(join_wide(x_lo, y, (z + dz) % 16), n), device_id_type=MESH_ID,
            ).start()

        @pl.when(dz == 0)
        def _():
            pltpu.make_async_copy(root, metric.at[slot], mrecv.at[0]).start()

        return carry

    lax.fori_loop(0, 8, send_metric, 0)
    pltpu.make_async_copy(raw.at[0, :, w], recv.at[120], rsem.at[120 // GROUP]).start()

    def send_raw(step, carry):
        peer = peer_at(step, w)

        @pl.when(peer != w)
        def _():
            pltpu.make_async_remote_copy(
                raw.at[0, :, peer], recv.at[step], ssem, rsem.at[step // GROUP], device_id=(peer, n),
                device_id_type=MESH_ID,
            ).start()

        return carry

    lax.fori_loop(0, 128, send_raw, 0)

    def part(side, k):
        start = side * half_rows + k % SHARES * rows
        return k // SHARES, pl.ds(pl.multiple_of(start, rows), rows)

    def send_own(k):
        for side, device in enumerate((x_next, x_prev)):
            at = part(side, k)
            pltpu.make_async_remote_copy(
                own.at[at[0], at[1]], relay.at[at[0], at[1]], own_sent, relay_in.at[side, k], device_id=device, device_id_type=MESH_ID
            ).start()

    def wait_for(ref, sem):
        pltpu.make_async_copy(ref, ref, sem).wait()

    def pass_on(k):
        for side, device in enumerate((x_next, x_prev)):
            at = part(side, k)
            wait_for(relay.at[at[0], at[1]], relay_in.at[side, k])
            pltpu.make_async_remote_copy(
                relay.at[at[0], at[1]], far.at[0, at[0], at[1]], relay_sent, near_in.at[side, k], device_id=device, device_id_type=MESH_ID
            ).start()

            @pl.when(jnp.logical_and(corner, x_lo == side))
            def _(side=side, at=at):
                pltpu.make_async_remote_copy(
                    relay.at[at[0], at[1]], far.at[1, at[0], at[1]], near_sent, next_in.at[side, k],
                    device_id=(join_wide(x_lo, 3, 15), n), device_id_type=MESH_ID,
                ).start()

    def send_near(k):
        for side in range(2):
            at = part(side, k)
            wait_for(far.at[0, at[0], at[1]], near_in.at[side, k])

            @pl.when(jnp.logical_or(jnp.logical_not(corner), x_lo == side))
            def _(side=side, at=at):
                pltpu.make_async_remote_copy(
                    far.at[0, at[0], at[1]], far.at[1, at[0], at[1]], near_sent, next_in.at[side, k],
                    device_id=(ahead, n), device_id_type=MESH_ID,
                ).start()

    def send_next(k):
        for side in range(2):
            at = part(side, k)
            wait_for(far.at[1, at[0], at[1]], next_in.at[side, k])

            @pl.when(corner)
            def _(side=side, at=at):
                pltpu.make_async_remote_copy(
                    far.at[1, at[0], at[1]], transit.at[at[0], at[1]], next_sent, turn_in.at[side, k],
                    device_id=(turned, n), device_id_type=MESH_ID,
                ).start()

            @pl.when(jnp.logical_not(corner))
            def _(at=at):
                pltpu.make_async_remote_copy(
                    far.at[1, at[0], at[1]], far.at[2, at[0], at[1]], next_sent, last_in.at[k // SHARES], device_id=(ahead, n), device_id_type=MESH_ID
                ).start()

    def send_turned(k):
        for side in range(2):
            at = part(side, k)
            wait_for(transit.at[at[0], at[1]], turn_in.at[side, k])
            pltpu.make_async_remote_copy(
                transit.at[at[0], at[1]], far.at[2, at[0], at[1]], turn_sent, last_in.at[k // SHARES],
                device_id=(join_wide(x_lo, 3, 15), n), device_id_type=MESH_ID,
            ).start()

    line = metric.at[pl.ds(pl.multiple_of(x_lo * 64 + y * 16 + par * 8, 8), 8)]
    pltpu.make_async_copy(line, line, mrecv.at[0]).wait()
    for step in range(1, 4):
        pltpu.make_async_remote_copy(
            line, line, msend.at[1], mrecv.at[1],
            device_id=(join_wide(x_lo, (y + step) % 4, z), n), device_id_type=MESH_ID,
        ).start()
    three = metric.at[pl.ds(0, 24)]
    pltpu.make_async_copy(three, three, mrecv.at[1]).wait()
    copies = []
    for row in range(4):
        span_ref = metric.at[pl.ds(pl.multiple_of(x_lo * 64 + row * 16 + par * 8, 8), 8)]
        copies.append(pltpu.make_async_remote_copy(
            span_ref, span_ref, msend.at[2], mrecv.at[2],
            device_id=(join_wide(1 - x_lo, y, z), n), device_id_type=MESH_ID,
        ))
    for copy in copies:
        copy.start()
    four = metric.at[pl.ds(0, 32)]
    pltpu.make_async_copy(four, four, mrecv.at[2]).wait()
    for row in range(8):
        span_ref = metric.at[pl.ds(pl.multiple_of(row * 16 + par * 8, 8), 8)]
        pltpu.make_async_remote_copy(
            span_ref, span_ref, msend.at[3], mrecv.at[3], device_id=sibling, device_id_type=MESH_ID
        ).start()
    eight = metric.at[pl.ds(0, 64)]
    pltpu.make_async_copy(eight, eight, mrecv.at[3]).wait()

    partner = (n + 2) % 4
    column[...] = jnp.broadcast_to(vir[pl.ds(n, 1), :], (128, nvir)).T
    partner_row = vir[pl.ds(partner, 1), :]
    dens[...] = jnp.zeros_like(dens)

    def reorder(step, carry):
        turn, side = 15 - step // 8, step % 8
        half = (turn + 1) // 2
        dz = jnp.where(turn % 2 == 1, 16 - half, half)
        source = join_wide((x_lo + side // 4) % 2, (y + 4 - side % 4) % 4, (z + dz) % 16)
        arranged[step] = metric[slot_of(source)]
        return carry

    lax.fori_loop(0, 128, reorder, 0)
    for g in range(128 // GROUP):
        for q in range(5):
            root_rows[q * GROUP : (q + 1) * GROUP, :] = arranged[g * GROUP : (g + 1) * GROUP, q, :]
        root_t[g] = root_rows[...].T

    def fill_table(s):
        there = (w + s) % 128
        for i in range(2):
            for j in range(2):
                level = occ[i, kpoint[n, w]] + occ[j, kpoint[partner, there]]
                alive = jnp.where(i < count[n, w], 1.0, 0.0) * jnp.where(j < count[partner, there], 1.0, 0.0)

                def some_rows(k, carry, i=i, j=j, level=level, alive=alive):
                    at = pl.multiple_of(k * 64, 64)
                    left = level - column[pl.ds(at, 64), :]
                    for c in range(nvir // 128):
                        gap = left - partner_row[:, c * 128 : (c + 1) * 128]
                        table[s, pl.ds(i * nvir + at, 64), j * nvir + c * 128 : j * nvir + (c + 1) * 128] = alive / gap
                    return carry

                lax.fori_loop(0, nvir // 64, some_rows, 0)

    def table_of(k, carry):
        fill_table(k)
        return carry

    lax.fori_loop(0, WINDOW, table_of, 0)
    for g in range(128 // GROUP):
        arrived = recv.at[pl.ds(g * GROUP, GROUP)]
        wait_for(arrived, rsem.at[g])
        for o in range(2):
            cols = slice(o * nvir, (o + 1) * nvir)
            for q in range(5):
                rows_in[q * GROUP : (q + 1) * GROUP, cols] = recv[g * GROUP : (g + 1) * GROUP, q, o, :]
            for k in range(5):
                at = slice(k * aux // 5, (k + 1) * aux // 5)
                term = jnp.dot(root_t[g, at, :], rows_in[:, cols], preferred_element_type=jnp.float32)
                if g == 0:
                    total[at, cols] = term
                elif g < 128 // GROUP - 1:
                    total[at, cols] += term
                else:
                    own[o, at, :] = (total[at, cols] + term).astype(own.dtype)
            if g == 128 // GROUP - 1 and o == 0:
                for k in range(AHEAD):
                    send_own(k)
    for o in range(2):
        own_t[o * nvir : (o + 1) * nvir, :] = own[o].T
    total[...] = jnp.zeros_like(total)

    def in_turn(k, action):
        @pl.when(jnp.logical_and(k >= 0, k < CHUNKS))
        def _():
            action(k)

    def round_of(k, carry):
        in_turn(k, pass_on)
        in_turn(k + AHEAD, send_own)
        in_turn(k - NEAR_LAG, send_near)
        in_turn(k - NEXT_LAG, send_next)

        @pl.when(corner)
        def _():
            in_turn(k - NEXT_LAG - 1, send_turned)

        return carry

    lax.fori_loop(0, CHUNKS + NEXT_LAG + 1, round_of, 0)

    def add_gamma(s):
        for i in range(2):
            cols = slice(i * nvir, (i + 1) * nvir)
            for j in range(2):
                total[:, cols] += lax.dot_general(
                    far[s, j], mix[i, :, j * nvir : (j + 1) * nvir], (((1,), (1,)), ((), ())),
                    preferred_element_type=jnp.float32,
                )

    def window_step(s, carry):
        for j in range(2):
            cols = slice(j * nvir, (j + 1) * nvir)

            @pl.when(s == WINDOW - 1)
            def _(j=j, cols=cols):
                wait_for(far.at[2, j], last_in.at[j])

            for i in range(2):
                left = own_t[i * nvir : (i + 1) * nvir, :]
                product = jnp.dot(left, far[s, j], preferred_element_type=jnp.float32)
                amplitude = product * table[s, i * nvir : (i + 1) * nvir, cols]
                half = amplitude.astype(jnp.bfloat16)
                amp[i, :, cols] = half
                mixed = 2.0 * amplitude - half.T.astype(jnp.float32)
                mix[i, :, cols] = mixed.astype(jnp.bfloat16)
        for i in range(2):
            dens[...] += lax.dot_general(
                mix[i], amp[i], (((1,), (1,)), ((), ())), preferred_element_type=jnp.float32
            )

        @pl.when(s < WINDOW - 1)
        def _():
            add_gamma(s)

        return carry

    lax.fori_loop(0, WINDOW, window_step, 0)

    span = nvir // 8

    def share(of_core, row):
        return dens.at[pl.ds(pl.multiple_of(of_core * 4 * span + row * span, span), span)]

    order = [(y + step) % 4 for step in (2, 1, 3, 0)]
    for row in order:
        pltpu.make_async_remote_copy(
            share(1 - core, row), core_in.at[row], dsend.at[0], core_got.at[row],
            device_id=sibling, device_id_type=MESH_ID,
        ).start()
    for step, row in zip((2, 1, 3), order):
        wait_for(core_in.at[row], core_got.at[row])
        y_out[row] = (share(core, row)[...] + core_in[row]).astype(y_out.dtype)
        pltpu.make_async_remote_copy(
            y_out.at[row], y_in.at[step - 1], dsend.at[1], drecv.at[1],
            device_id=(join_wide(x_lo, row, z), n), device_id_type=MESH_ID,
        ).start()
    add_gamma(WINDOW - 1)
    wait_for(core_in.at[y], core_got.at[y])
    mine = share(core, y)[...] + core_in[y]
    wait_for(y_in, drecv.at[1])
    z_sum[...] = mine + add_up(y_in, 3)
    for k in range(16):
        for r in range(3):
            for c in range(3):
                z_all[k, 3 * r + c : 3 * r + c + 1, :] = z_sum[3 * k + r : 3 * k + r + 1, c * 128 : (c + 1) * 128]
    z_out[...] = z_all[...].astype(z_out.dtype)
    for step in sorted(range(1, 16), key=lambda k: abs(k - 8)):
        to = (z + step) % 16
        pltpu.make_async_remote_copy(
            z_out.at[to], z_in.at[step - 1], dsend.at[2], drecv.at[2],
            device_id=(join_wide(x_lo, y, to), n), device_id_type=MESH_ID,
        ).start()
    for i in range(2):
        leaving[:, i, :] = total[:, i * nvir : (i + 1) * nvir].astype(gamma.dtype)
    wait_for(z_in, drecv.at[2])
    x_out[...] = z_all[z] + add_up(z_in, 15)
    for device in targets:
        here = jnp.logical_and(device[0] == w, device[1] == n)

        @pl.when(here)
        def _():
            pltpu.make_async_copy(x_out, x_in.at[x], drecv.at[3]).start()

        @pl.when(jnp.logical_not(here))
        def _(device=device):
            pltpu.make_async_remote_copy(
                x_out, x_in.at[x], dsend.at[3], drecv.at[3], device_id=device, device_id_type=MESH_ID
            ).start()

    pltpu.make_async_copy(leaving, gamma, left_sem).start()
    wait_for(x_in, drecv.at[3])
    piece[...] = add_up(x_in, 4) * (1.0 / (4 * 128 * nvir))

    pltpu.make_async_copy(leaving, gamma, left_sem).wait()
    wait_for(own, own_sent)
    wait_for(own, relay_sent)
    wait_for(own, near_sent)
    wait_for(own, next_sent)

    @pl.when(corner)
    def _():
        wait_for(transit, turn_sent)

    wait_for(core_in, dsend.at[0])
    wait_for(y_in, dsend.at[1])
    wait_for(z_in, dsend.at[2])

    @pl.when(at_home)
    def _():
        wait_for(x_in.at[pl.ds(0, 3)], dsend.at[3])

    @pl.when(jnp.logical_not(at_home))
    def _():
        wait_for(x_in, dsend.at[3])

    @pl.when(core == 0)
    def _():
        span_ref = metric.at[pl.ds(0, 7)]
        pltpu.make_async_copy(span_ref, span_ref, msend.at[0]).wait()

    @pl.when(core == 1)
    def _():
        span_ref = metric.at[pl.ds(0, 8)]
        pltpu.make_async_copy(span_ref, span_ref, msend.at[0]).wait()

    pltpu.make_async_copy(three, three, msend.at[1]).wait()
    pltpu.make_async_copy(four, four, msend.at[2]).wait()
    pltpu.make_async_copy(eight, eight, msend.at[3]).wait()
    others = recv.at[pl.ds(0, 127)]
    pltpu.make_async_copy(others, others, ssem).wait()


def window_call(raw, root, vir, occ, kpoint, count):
    aux = root.shape[1]
    width = 2 * vir.shape[1]
    nvir = vir.shape[1]
    bf16, f32 = jnp.bfloat16, jnp.float32
    dma = pltpu.SemaphoreType.DMA
    vmem = pl.BlockSpec(memory_space=pltpu.VMEM)
    smem = pl.BlockSpec(memory_space=pltpu.SMEM)
    return pl.pallas_call(
        window_kernel,
        name="window",
        out_shape=(jax.ShapeDtypeStruct((aux, 2, width // 2), bf16), jax.ShapeDtypeStruct((9, 128), f32)),
        in_specs=[vmem, vmem, vmem, smem, smem, smem],
        out_specs=(pl.BlockSpec(memory_space=pl.ANY), vmem),
        scratch_shapes=[
            pltpu.VMEM((aux, 2, nvir), bf16),
            pltpu.VMEM((128,) + raw.shape[1:2] + raw.shape[3:], bf16),
            pltpu.VMEM((128,) + root.shape, bf16),
            pltpu.VMEM((128,) + root.shape, bf16),
            pltpu.VMEM((5 * GROUP, aux), bf16),
            pltpu.VMEM((128 // GROUP, aux, 5 * GROUP), bf16),
            pltpu.VMEM((5 * GROUP, width), bf16),
            pltpu.VMEM((2, aux, nvir), bf16),
            pltpu.VMEM((width, aux), bf16),
            pltpu.VMEM((2, aux, nvir), bf16),
            pltpu.VMEM((2, aux, nvir), bf16),
            pltpu.VMEM((WINDOW, 2, aux, nvir), bf16),
            pltpu.VMEM((WINDOW, width, width), f32),
            pltpu.VMEM((nvir, 128), f32),
            pltpu.VMEM((aux, width), f32),
            pltpu.VMEM((nvir, nvir), f32),
            pltpu.VMEM((2, nvir, width), bf16),
            pltpu.VMEM((2, nvir, width), bf16),
            pltpu.VMEM((4, nvir // 8, nvir), f32),
            pltpu.VMEM((4, nvir // 8, nvir), bf16),
            pltpu.VMEM((3, nvir // 8, nvir), bf16),
            pltpu.VMEM((nvir // 8, nvir), f32),
            pltpu.VMEM((16, 9, 128), f32),
            pltpu.VMEM((16, 9, 128), bf16),
            pltpu.VMEM((15, 9, 128), bf16),
            pltpu.VMEM((9, 128), f32),
            pltpu.VMEM((4, 9, 128), f32),
            dma,
            dma((2, CHUNKS)),
            dma,
            dma((2, CHUNKS)),
            dma,
            dma((2, CHUNKS)),
            dma,
            dma((2,)),
            dma((2, CHUNKS)),
            dma,
            dma((4,)),
            dma((4,)),
            dma((4,)),
            dma,
            dma((128 // GROUP,)),
            dma((4,)),
            dma((4,)),
            dma,
        ],
        compiler_params=pltpu.CompilerParams(
            collective_id=0, has_side_effects=True, vmem_limit_bytes=60000 * 1024
        ),
    )(raw, root, vir, occ, kpoint, count)


def finish_kernel(gamma, piece, gamma_out, density, sem):
    copy = pltpu.make_async_copy(gamma, gamma_out, sem)
    copy.start()
    n = lax.axis_index("narrow")
    for k in range(4):

        @pl.when(n == k)
        def _(k=k):
            cut = 32 * k
            for r in range(3):
                row = piece[2 * k + r : 2 * k + r + 1, cut:]
                if cut and 2 * k + r + 1 < 9:
                    row = jnp.concatenate([row, piece[2 * k + r + 1 : 2 * k + r + 2, :cut]], axis=1)
                size = 128 if r < 2 else 32
                density[r * 128 : r * 128 + size] = row[0, :size]

    copy.wait()


def finish(gamma, piece):
    vmem = pl.BlockSpec(memory_space=pltpu.VMEM)
    return pl.pallas_call(
        finish_kernel,
        name="finish",
        out_shape=(jax.ShapeDtypeStruct(gamma.shape, gamma.dtype), jax.ShapeDtypeStruct((288,), jnp.float32)),
        in_specs=[vmem, vmem],
        out_specs=(pl.BlockSpec(memory_space=pl.ANY), vmem),
        scratch_shapes=[pltpu.SemaphoreType.DMA],
    )(gamma, piece)


def shards(raw_ints, metric_root, occ_energy, vir_energy, block_kpoint, occ_count):
    nvir = raw_ints.shape[4]
    aux = metric_root.shape[1]
    gamma, piece = window_call(raw_ints, metric_root, vir_energy, occ_energy.T, block_kpoint, occ_count)
    gamma, density = finish(gamma, piece)
    return gamma.reshape(1, aux, 1, 2, nvir), density


def solution(mesh):
    placed = (P("narrow", "wide", None, None, None), P("wide", None), P(), P(), P(), P())
    return jax.shard_map(
        shards,
        mesh=mesh,
        in_specs=placed,
        out_specs=(P("narrow", None, "wide", None, None), P(("wide", "narrow"))),
        check_vma=False,
    )
```
